256 devices in a mesh: elem: 256 (over z, y, x, core).
Axes of the slice: x: 4, y: 4, z: 8, core: 2. Of those that a mesh axis runs over, the one named last changes fastest.
Arguments:
- moment_fields: float32 [3, 512, 32768], P(None, None, 'elem'), may hold values from -6 to 6
- adjoint_fields: float32 [3, 512, 32768], P(None, None, 'elem'), may hold values from -6 to 6
- velocity: float32 [3, 512, 32768], P(None, None, 'elem'), may hold values from -12 to 12
- mass_weights: float32 [512, 32768], P(None, 'elem'), may hold values from 0.5 to 2
- diffusivity: float32 [3], replicated, may hold values from 0.1 to 0.5
- numbering: int32 [32768], P('elem'), may hold values from 0 to 32767, as said below
Outputs:
- moments: float32 [3, 512, 32768], P(None, None, 'elem')
- sensitivities: float32 [3, 512, 32768], P(None, None, 'elem')
The draws below stay inside these ranges and needn't reach their ends.
Inputs may be any that keep to these rules, and one draw needn't show every extreme that they name: `numbering`: rows d * 128 to (d + 1) * 128 - 1 hold, in some order, each of the numbers c * 128 to (c + 1) * 128 - 1 once, where c = (d + 32) % 256.
All inputs are finite; a program needn't handle non-finite values.
Results may differ from the reference program's by a relative error of at most 0.0001.
Values sent between devices are 32-bit elements; how exact they have to be, the bound alone decides.
A program may use at most 64 MiB of HBM per device.

```python
import math
import jax
import jax.numpy as jnp
import numpy as np
from jax import lax

FIELDS = 3
NODES = 512
DA = 4
EZ = 128
DB = 64
ELEMENTS = 32768


def draw_numbering(key, part):
    column_keys = jax.random.split(key, DA * DB)
    orderings = jax.vmap(lambda one_key: jax.random.permutation(one_key, EZ))(column_keys).astype(jnp.int32)
    device_index = lax.iota(jnp.int32, DA * DB)
    column_index = (device_index + DB // 2) % (DA * DB)
    offsets = column_index[:, None] * EZ
    return (orderings + offsets).reshape(-1).astype(jnp.int32)


def block_levels(own_key, extent, cuts, low, top_value):
    loudness, own = 1.0, jax.random.fold_in(own_key, 6)
    for position, blocks in cuts:
        draws = jnp.exp(jax.random.uniform(jax.random.fold_in(own, position), (blocks,), jnp.float32, low / len(cuts), top_value / len(cuts)))
        loudness = loudness * jnp.repeat(draws, extent[position] // blocks).reshape([-1 if axis == position else 1 for axis in range(len(extent))])
    return loudness


def normal_values(key, extent, width, bound, cuts=(), held_as=jnp.bfloat16):
    array = width * jax.random.normal(key, extent, jnp.float32)
    if cuts:
        array = array * block_levels(key, extent, cuts, -0.22, 0.18)
    return jnp.clip(array, -bound, bound).astype(held_as)


def setup_inputs(seed: int = 0) -> dict:
    key_list = jax.random.split(jax.random.key(seed), 7)
    moment_fields = normal_values(key_list[0], (FIELDS, NODES, ELEMENTS), 1.0, 6.0, ((2, 256),), jnp.float32)
    adjoint_fields = normal_values(key_list[1], (FIELDS, NODES, ELEMENTS), 1.0, 6.0, ((2, 256),), jnp.float32)
    velocity = normal_values(key_list[2], (3, NODES, ELEMENTS), 3.0, 12.0, ((2, 256),), jnp.float32)
    mass_weights = jnp.clip(jnp.exp(math.log(2.0) - 1.3862944 * jax.random.uniform(key_list[3], (NODES, ELEMENTS), jnp.float32) ** block_levels(key_list[3], (NODES, ELEMENTS), ((1, 256),), -0.2, 0.2)), 0.5, 2.0)
    diffusivity = jnp.clip(jnp.exp(jax.random.uniform(key_list[4], (FIELDS,), jnp.float32, math.log(0.1), math.log(0.5))), 0.1, 0.5)
    numbering = draw_numbering(jax.random.fold_in(key_list[6], 71), 0)
    return {"moment_fields": moment_fields, "adjoint_fields": adjoint_fields, "velocity": velocity, "mass_weights": mass_weights, "diffusivity": diffusivity, "numbering": numbering}


time_step = 0.001
highest = lax.Precision.HIGHEST


def gll_tables():
    points = [-1.0, -0.8717401485096066, -0.5917001814331423, -0.2092992179024789, 0.2092992179024789, 0.5917001814331423, 0.8717401485096066, 1.0]
    weights = [0.03571428571428571, 0.21070422714350603, 0.3411226924835044, 0.4124587946587038, 0.4124587946587038, 0.3411226924835044, 0.21070422714350603, 0.03571428571428571]
    barycentric = []
    for left_index in range(8):
        product = 1.0
        for right_index in range(8):
            if right_index != left_index:
                product = product * (points[left_index] - points[right_index])
        barycentric.append(1.0 / product)
    derivative = np.zeros((8, 8))
    for left_index in range(8):
        row_total = 0.0
        for right_index in range(8):
            if left_index != right_index:
                entry = (barycentric[right_index] / barycentric[left_index]) / (points[left_index] - points[right_index])
                derivative[left_index, right_index] = entry
                row_total = row_total + entry
        derivative[left_index, left_index] = -row_total
    return jnp.asarray(derivative, dtype=jnp.float32), jnp.asarray(weights, dtype=jnp.float32)


def gradient(quantity, derivative):
    along_i = jnp.einsum('pi,gijke->gpjke', derivative, quantity, precision=highest)
    along_j = jnp.einsum('pj,gijke->gipke', derivative, quantity, precision=highest)
    along_k = jnp.einsum('pk,gijke->gijpe', derivative, quantity, precision=highest)
    return along_i, along_j, along_k


def transposed(quantity, derivative, direction):
    if direction == 0:
        return jnp.einsum('ip,gijke->gpjke', derivative, quantity, precision=highest)
    if direction == 1:
        return jnp.einsum('jp,gijke->gipke', derivative, quantity, precision=highest)
    return jnp.einsum('kp,gijke->gijpe', derivative, quantity, precision=highest)


def forward_terms(quantity, velocity, mass_cube, diffusivity, derivative):
    gradients = gradient(quantity, derivative)
    advect = velocity[0] * gradients[0] + velocity[1] * gradients[1] + velocity[2] * gradients[2]
    diffuse = transposed(mass_cube * gradients[0], derivative, 0)
    diffuse = diffuse + transposed(mass_cube * gradients[1], derivative, 1)
    diffuse = diffuse + transposed(mass_cube * gradients[2], derivative, 2)
    return -(mass_cube * advect) - diffusivity[:, None, None, None, None] * diffuse


def adjoint_terms(quantity, velocity, mass_cube, diffusivity, derivative):
    gradients = gradient(quantity, derivative)
    scaled = diffusivity[:, None, None, None, None]
    summed = transposed(mass_cube * (velocity[0] * quantity + scaled * gradients[0]), derivative, 0)
    summed = summed + transposed(mass_cube * (velocity[1] * quantity + scaled * gradients[1]), derivative, 1)
    summed = summed + transposed(mass_cube * (velocity[2] * quantity + scaled * gradients[2]), derivative, 2)
    return -summed


def global_numbers(numbering):
    pencil = numbering // EZ
    height = numbering % EZ
    slab_row = pencil // DB
    slab_place = pencil % DB
    node_index = lax.iota(jnp.int32, 512)
    node_i = (node_index // 64)[:, None]
    node_j = ((node_index // 8) % 8)[:, None]
    node_k = (node_index % 8)[:, None]
    coord_x = 7 * slab_row[None, :] + node_i
    coord_y = 7 * slab_place[None, :] + node_j
    coord_z = 7 * height[None, :] + node_k
    return ((coord_x * (7 * DB + 1) + coord_y) * (7 * EZ + 1) + coord_z).astype(jnp.int32)


def assemble(values, global_node):
    count = values.shape[0]
    flattened = values.reshape(count, -1).T
    segment_ids = global_node.reshape(-1)
    totals = jax.ops.segment_sum(flattened, segment_ids, num_segments=(7 * DA + 1) * (7 * DB + 1) * (7 * EZ + 1))
    return totals[segment_ids].T.reshape(values.shape)


def reference(moment_fields, adjoint_fields, velocity, mass_weights, diffusivity, numbering):
    derivative, weights = gll_tables()
    elements = numbering.shape[0]
    count = moment_fields.shape[0]
    global_node = global_numbers(numbering)
    weight_cube = weights[:, None, None] * weights[None, :, None] * weights[None, None, :]
    mass_cube = mass_weights.reshape(8, 8, 8, elements) * weight_cube[:, :, :, None]
    mass_sum = assemble(mass_cube[None], global_node)[0]
    flow = velocity.reshape(3, 8, 8, 8, elements)
    fields_now = moment_fields.reshape(count, 8, 8, 8, elements)
    for step_index in range(2):
        terms = forward_terms(fields_now, flow, mass_cube, diffusivity, derivative)
        fields_now = fields_now + time_step * assemble(terms, global_node) / mass_sum
    adjoint_now = adjoint_fields.reshape(count, 8, 8, 8, elements)
    for step_index in range(2):
        gathered = assemble(adjoint_now / mass_sum, global_node)
        adjoint_now = adjoint_now + time_step * adjoint_terms(gathered, flow, mass_cube, diffusivity, derivative)
    return fields_now.reshape(count, 512, elements), adjoint_now.reshape(count, 512, elements)
```

```python
import functools

import jax
import jax.numpy as jnp
import numpy as np
from jax import lax
from jax.experimental import pallas as pl
from jax.experimental.pallas import tpu as pltpu
from jax.sharding import PartitionSpec as P

DA = 4

time_step = 0.001


def gll_tables():
    points = [
        -1.0,
        -0.8717401485096066,
        -0.5917001814331423,
        -0.2092992179024789,
        0.2092992179024789,
        0.5917001814331423,
        0.8717401485096066,
        1.0,
    ]
    weights = [
        0.03571428571428571,
        0.21070422714350603,
        0.3411226924835044,
        0.4124587946587038,
        0.4124587946587038,
        0.3411226924835044,
        0.21070422714350603,
        0.03571428571428571,
    ]
    barycentric = []
    for left_index in range(8):
        product = 1.0
        for right_index in range(8):
            if right_index != left_index:
                product = product * (points[left_index] - points[right_index])
        barycentric.append(1.0 / product)
    derivative = np.zeros((8, 8))
    for left_index in range(8):
        row_total = 0.0
        for right_index in range(8):
            if left_index != right_index:
                entry = (
                    barycentric[right_index]
                    / barycentric[left_index]
                    / (points[left_index] - points[right_index])
                )
                derivative[left_index, right_index] = entry
                row_total = row_total + entry
        derivative[left_index, left_index] = -row_total
    return derivative.astype(np.float32), np.asarray(weights, dtype=np.float32)


DM, WEIGHTS = gll_tables()
DMC = [[float(DM[p, q]) for q in range(8)] for p in range(8)]


def shift_tables():
    fwd = np.zeros((8, 8, 128), np.float32)
    bwd = np.zeros((8, 8, 128), np.float32)
    for s in range(8):
        for p in range(8):
            fwd[s, p, :] = DM[p, (p - s) % 8]
            bwd[s, p, :] = DM[(p - s) % 8, p]
    return np.concatenate([fwd, bwd], axis=0)


def along_major(v, axis, transpose):
    parts = []
    for p in range(8):
        acc = None
        for q in range(8):
            c = DMC[q][p] if transpose else DMC[p][q]
            term = c * (v[q] if axis == 0 else v[:, q])
            acc = term if acc is None else acc + term
        parts.append(acc)
    return jnp.stack(parts, axis=axis)


def along_sublane(v, tab_ref, base):
    acc = None
    for s in range(8):
        rolled = v if s == 0 else pltpu.roll(v, s, 2)
        term = tab_ref[base + s] * rolled
        acc = term if acc is None else acc + term
    return acc


def gradients(v, tab_ref):
    return (
        along_major(v, 0, False),
        along_major(v, 1, False),
        along_sublane(v, tab_ref, 0),
    )


def transposed(v, tab_ref, direction):
    if direction == 0:
        return along_major(v, 0, True)
    if direction == 1:
        return along_major(v, 1, True)
    return along_sublane(v, tab_ref, 8)


def forward_terms(q, flow, mass, kappa, tab_ref):
    g = gradients(q, tab_ref)
    advect = flow[0] * g[0] + flow[1] * g[1] + flow[2] * g[2]
    diffuse = transposed(mass * g[0], tab_ref, 0)
    diffuse = diffuse + transposed(mass * g[1], tab_ref, 1)
    diffuse = diffuse + transposed(mass * g[2], tab_ref, 2)
    return -(mass * advect) - kappa * diffuse


def adjoint_terms(q, flow, mass, kappa, tab_ref):
    g = gradients(q, tab_ref)
    summed = transposed(mass * (flow[0] * q + kappa * g[0]), tab_ref, 0)
    summed = summed + transposed(mass * (flow[1] * q + kappa * g[1]), tab_ref, 1)
    summed = summed + transposed(mass * (flow[2] * q + kappa * g[2]), tab_ref, 2)
    return -summed


def z_assemble(v):
    shape = v.shape
    sub = lax.broadcasted_iota(jnp.int32, shape, 2)
    lane = lax.broadcasted_iota(jnp.int32, shape, 3)
    below = pltpu.roll(pltpu.roll(v, 1, 2), 1, 3)
    above = pltpu.roll(pltpu.roll(v, 7, 2), 127, 3)
    zero = jnp.zeros_like(v)
    v = v + jnp.where((sub == 0) & (lane > 0), below, zero)
    return v + jnp.where((sub == 7) & (lane < 127), above, zero)


def kernel(
    ndev,
    cols,
    fld_ref,
    adj_ref,
    vel_ref,
    mass_ref,
    tab_ref,
    kap_ref,
    out_f_ref,
    out_a_ref,
    x1,
    x2,
    x3,
    ms_ref,
    f1_ref,
    a1_ref,
    sj1,
    rj1,
    si1,
    ri1,
    sj2,
    rj2,
    si2,
    ri2,
    sj3,
    rj3,
    si3,
    ri3,
    ssem,
    rsem,
):
    me = lax.axis_index("elem")
    column = (me + cols // 2) % ndev
    place = column % cols
    row = column // cols
    right = (me + 1) % ndev
    left = (me + ndev - 1) % ndev
    up = (me + cols) % ndev
    down = (me + ndev - cols) % ndev
    has_right = place < cols - 1
    has_left = place > 0
    has_up = row < DA - 1
    has_down = row > 0

    barrier = pltpu.get_barrier_semaphore()
    for nb in (left, right, up, down):
        pl.semaphore_signal(barrier, inc=1, device_id=(nb,), device_id_type=pl.DeviceIdType.MESH)
    pl.semaphore_wait(barrier, 4)

    def exchange(x, nf, rnd, sj, rj, si, ri):
        for f in range(nf):
            x[f] = z_assemble(x[f])
        for f in range(nf):
            sj[0, f] = x[f, :, 0]
            sj[1, f] = x[f, :, 7]

        def pair(s_buf, r_buf, d, hi, lo, has_hi, has_lo, fixup):
            c_hi = pltpu.make_async_remote_copy(
                s_buf.at[1], r_buf.at[0], ssem.at[rnd, d, 1], rsem.at[rnd, d, 0],
                device_id=(hi,), device_id_type=pl.DeviceIdType.MESH,
            )
            c_lo = pltpu.make_async_remote_copy(
                s_buf.at[0], r_buf.at[1], ssem.at[rnd, d, 0], rsem.at[rnd, d, 1],
                device_id=(lo,), device_id_type=pl.DeviceIdType.MESH,
            )

            @pl.when(has_hi)
            def _():
                c_hi.start()

            @pl.when(has_lo)
            def _():
                c_lo.start()

            @pl.when(has_hi)
            def _():
                c_hi.wait_send()
                c_lo.wait_recv()
                fixup(7, r_buf.at[1])

            @pl.when(has_lo)
            def _():
                c_lo.wait_send()
                c_hi.wait_recv()
                fixup(0, r_buf.at[0])

        def fix_j(side, buf):
            for f in range(nf):
                x[f, :, side] = x[f, :, side] + buf[f]

        pair(sj, rj, 0, right, left, has_right, has_left, fix_j)

        for f in range(nf):
            si[0, f] = x[f, 0]
            si[1, f] = x[f, 7]

        def fix_i(side, buf):
            for f in range(nf):
                x[f, side] = x[f, side] + buf[f]

        pair(si, ri, 1, up, down, has_up, has_down, fix_i)

    def flow():
        return (vel_ref[0], vel_ref[1], vel_ref[2])

    x1[0] = mass_ref[...]

    def r1_body(f, c):
        x1[f + 1] = forward_terms(fld_ref[f], flow(), mass_ref[...], kap_ref[f], tab_ref)
        return c

    lax.fori_loop(0, 3, r1_body, 0)
    exchange(x1, 4, 0, sj1, rj1, si1, ri1)
    ms_ref[...] = x1[0]

    def f1_body(f, c):
        f1_ref[f] = fld_ref[f] + time_step * x1[f + 1] / ms_ref[...]
        x2[f + 3] = adj_ref[f] / ms_ref[...]
        return c

    lax.fori_loop(0, 3, f1_body, 0)

    def r2_body(f, c):
        x2[f] = forward_terms(f1_ref[f], flow(), mass_ref[...], kap_ref[f], tab_ref)
        return c

    lax.fori_loop(0, 3, r2_body, 0)
    exchange(x2, 6, 1, sj2, rj2, si2, ri2)

    def a1_body(f, c):
        out_f_ref[f] = f1_ref[f] + time_step * x2[f] / ms_ref[...]
        a1 = adj_ref[f] + time_step * adjoint_terms(x2[f + 3], flow(), mass_ref[...], kap_ref[f], tab_ref)
        a1_ref[f] = a1
        x3[f] = a1 / ms_ref[...]
        return c

    lax.fori_loop(0, 3, a1_body, 0)

    exchange(x3, 3, 2, sj3, rj3, si3, ri3)

    def a2_body(f, c):
        out_a_ref[f] = a1_ref[f] + time_step * adjoint_terms(x3[f], flow(), mass_ref[...], kap_ref[f], tab_ref)
        return c

    lax.fori_loop(0, 3, a2_body, 0)


def fused(fields, adjoint, flow, mass, table, kappa, ndev, cols):
    cube = (8, 8, 8, 128)
    f32 = jnp.float32
    vmem = pl.BlockSpec(memory_space=pltpu.VMEM)
    smem = pl.BlockSpec(memory_space=pltpu.SMEM)
    scratch = [
        pltpu.VMEM((4,) + cube, f32),
        pltpu.VMEM((6,) + cube, f32),
        pltpu.VMEM((3,) + cube, f32),
        pltpu.VMEM(cube, f32),
        pltpu.VMEM((3,) + cube, f32),
        pltpu.VMEM((3,) + cube, f32),
    ]
    for nf in (4, 6, 3):
        for _ in range(4):
            scratch.append(pltpu.VMEM((2, nf, 8, 8, 128), f32))
    scratch += [pltpu.SemaphoreType.DMA((3, 2, 2)), pltpu.SemaphoreType.DMA((3, 2, 2))]
    return pl.pallas_call(
        functools.partial(kernel, ndev, cols),
        out_shape=(jax.ShapeDtypeStruct((3,) + cube, f32), jax.ShapeDtypeStruct((3,) + cube, f32)),
        in_specs=[vmem, vmem, vmem, vmem, vmem, smem],
        out_specs=(vmem, vmem),
        scratch_shapes=scratch,
        compiler_params=pltpu.CompilerParams(
            collective_id=0, has_side_effects=True, vmem_limit_bytes=60 * 1024 * 1024
        ),
    )(fields, adjoint, flow, mass, table, kappa)


def shards(moment_fields, adjoint_fields, velocity, mass_weights, diffusivity, numbering):
    height_count = numbering.shape[0]
    count = moment_fields.shape[0]
    ndev = lax.axis_size("elem")
    cols = ndev // DA
    height = numbering % height_count
    slot_index = lax.iota(jnp.int32, height_count)
    inverse = jnp.sum(
        jnp.where(height[:, None] == slot_index[None, :], slot_index[:, None], 0), axis=0
    )
    weights = jnp.asarray(WEIGHTS)
    weight_cube = weights[:, None, None] * weights[None, :, None] * weights[None, None, :]
    mass_cube = (
        jnp.take(mass_weights, inverse, axis=-1).reshape(8, 8, 8, height_count)
        * weight_cube[:, :, :, None]
    )
    flow = jnp.take(velocity, inverse, axis=-1).reshape(3, 8, 8, 8, height_count)
    fields_now = jnp.take(moment_fields, inverse, axis=-1).reshape(count, 8, 8, 8, height_count)
    adjoint_now = jnp.take(adjoint_fields, inverse, axis=-1).reshape(count, 8, 8, 8, height_count)
    table = jnp.asarray(shift_tables())
    out_f, out_a = fused(fields_now, adjoint_now, flow, mass_cube, table, diffusivity, ndev, cols)
    moments = jnp.take(out_f.reshape(count, 512, height_count), height, axis=-1)
    sensitivities = jnp.take(out_a.reshape(count, 512, height_count), height, axis=-1)
    return (moments, sensitivities)


def solution(mesh):
    in_specs = (
        P(None, None, "elem"),
        P(None, None, "elem"),
        P(None, None, "elem"),
        P(None, "elem"),
        P(),
        P("elem"),
    )
    out_specs = (P(None, None, "elem"), P(None, None, "elem"))
    return jax.shard_map(shards, mesh=mesh, in_specs=in_specs, out_specs=out_specs, check_vma=False)
```

```python
import functools

import jax
import jax.numpy as jnp
import numpy as np
from jax import lax
from jax.experimental import pallas as pl
from jax.experimental.pallas import tpu as pltpu
from jax.sharding import PartitionSpec as P

DA = 4

time_step = 0.001


def gll_tables():
    points = [
        -1.0,
        -0.8717401485096066,
        -0.5917001814331423,
        -0.2092992179024789,
        0.2092992179024789,
        0.5917001814331423,
        0.8717401485096066,
        1.0,
    ]
    weights = [
        0.03571428571428571,
        0.21070422714350603,
        0.3411226924835044,
        0.4124587946587038,
        0.4124587946587038,
        0.3411226924835044,
        0.21070422714350603,
        0.03571428571428571,
    ]
    barycentric = []
    for left_index in range(8):
        product = 1.0
        for right_index in range(8):
            if right_index != left_index:
                product = product * (points[left_index] - points[right_index])
        barycentric.append(1.0 / product)
    derivative = np.zeros((8, 8))
    for left_index in range(8):
        row_total = 0.0
        for right_index in range(8):
            if left_index != right_index:
                entry = (
                    barycentric[right_index]
                    / barycentric[left_index]
                    / (points[left_index] - points[right_index])
                )
                derivative[left_index, right_index] = entry
                row_total = row_total + entry
        derivative[left_index, left_index] = -row_total
    return derivative.astype(np.float32), np.asarray(weights, dtype=np.float32)


DM, WEIGHTS = gll_tables()
DMC = [[float(DM[p, q]) for q in range(8)] for p in range(8)]


def shift_tables():
    fwd = np.zeros((8, 8, 128), np.float32)
    bwd = np.zeros((8, 8, 128), np.float32)
    for s in range(8):
        for p in range(8):
            fwd[s, p, :] = DM[p, (p - s) % 8]
            bwd[s, p, :] = DM[(p - s) % 8, p]
    return np.concatenate([fwd, bwd], axis=0)


def along_major(v, axis, transpose):
    parts = []
    for p in range(8):
        acc = None
        for q in range(8):
            c = DMC[q][p] if transpose else DMC[p][q]
            term = c * (v[q] if axis == 0 else v[:, q])
            acc = term if acc is None else acc + term
        parts.append(acc)
    return jnp.stack(parts, axis=axis)


def along_sublane(v, tab_ref, base):
    acc = None
    for s in range(8):
        rolled = v if s == 0 else pltpu.roll(v, s, 2)
        term = tab_ref[base + s] * rolled
        acc = term if acc is None else acc + term
    return acc


def gradients(v, tab_ref):
    return (
        along_major(v, 0, False),
        along_major(v, 1, False),
        along_sublane(v, tab_ref, 0),
    )


def transposed(v, tab_ref, direction):
    if direction == 0:
        return along_major(v, 0, True)
    if direction == 1:
        return along_major(v, 1, True)
    return along_sublane(v, tab_ref, 8)


def forward_terms(q, flow, mass, kappa, tab_ref):
    g = gradients(q, tab_ref)
    advect = flow[0] * g[0] + flow[1] * g[1] + flow[2] * g[2]
    diffuse = transposed(mass * g[0], tab_ref, 0)
    diffuse = diffuse + transposed(mass * g[1], tab_ref, 1)
    diffuse = diffuse + transposed(mass * g[2], tab_ref, 2)
    return -(mass * advect) - kappa * diffuse


def adjoint_terms(q, flow, mass, kappa, tab_ref):
    g = gradients(q, tab_ref)
    summed = transposed(mass * (flow[0] * q + kappa * g[0]), tab_ref, 0)
    summed = summed + transposed(mass * (flow[1] * q + kappa * g[1]), tab_ref, 1)
    summed = summed + transposed(mass * (flow[2] * q + kappa * g[2]), tab_ref, 2)
    return -summed


def z_assemble(v):
    shape = v.shape
    sub = lax.broadcasted_iota(jnp.int32, shape, 2)
    lane = lax.broadcasted_iota(jnp.int32, shape, 3)
    below = pltpu.roll(pltpu.roll(v, 1, 2), 1, 3)
    above = pltpu.roll(pltpu.roll(v, 7, 2), 127, 3)
    zero = jnp.zeros_like(v)
    v = v + jnp.where((sub == 0) & (lane > 0), below, zero)
    return v + jnp.where((sub == 7) & (lane < 127), above, zero)


def permute(x, pm):
    bf = jnp.bfloat16
    f32 = jnp.float32
    x1 = x.astype(bf)
    r1 = x - x1.astype(f32)
    x2 = r1.astype(bf)
    x3 = (r1 - x2.astype(f32)).astype(bf)
    y = jnp.dot(x1, pm, preferred_element_type=f32)
    y = y + jnp.dot(x2, pm, preferred_element_type=f32)
    return y + jnp.dot(x3, pm, preferred_element_type=f32)


def kernel(
    ndev,
    cols,
    fld_in,
    adj_in,
    vel_in,
    mass_in,
    tab_ref,
    pin_ref,
    pout_ref,
    kap_ref,
    out_f_in,
    out_a_in,
    fld_ref,
    adj_ref,
    vel_ref,
    mass_ref,
    out_f_ref,
    out_a_ref,
    x1,
    x2,
    x3,
    ms_ref,
    f1_ref,
    a1_ref,
    sj1,
    rj1,
    si1,
    ri1,
    sj2,
    rj2,
    si2,
    ri2,
    sj3,
    rj3,
    si3,
    ri3,
    ssem,
    rsem,
):
    me = lax.axis_index("elem")
    column = (me + cols // 2) % ndev
    place = column % cols
    row = column // cols
    right = (me + 1) % ndev
    left = (me + ndev - 1) % ndev
    up = (me + cols) % ndev
    down = (me + ndev - cols) % ndev
    has_right = place < cols - 1
    has_left = place > 0
    has_up = row < DA - 1
    has_down = row > 0

    barrier = pltpu.get_barrier_semaphore()
    for nb in (left, right, up, down):
        pl.semaphore_signal(barrier, inc=1, device_id=(nb,), device_id_type=pl.DeviceIdType.MESH)
    pl.semaphore_wait(barrier, 4)

    def sort_in(src_ref, dst_ref):
        dst_ref[...] = permute(src_ref[...], pin_ref[...]).reshape(dst_ref.shape)

    for f in range(3):
        sort_in(fld_in.at[f], fld_ref.at[f])
        sort_in(adj_in.at[f], adj_ref.at[f])
        sort_in(vel_in.at[f], vel_ref.at[f])
    sort_in(mass_in, mass_ref)

    def exchange(x, nf, rnd, sj, rj, si, ri):
        for f in range(nf):
            x[f] = z_assemble(x[f])
        for f in range(nf):
            sj[0, f] = x[f, :, 0]
            sj[1, f] = x[f, :, 7]

        def pair(s_buf, r_buf, d, hi, lo, has_hi, has_lo, fixup):
            c_hi = pltpu.make_async_remote_copy(
                s_buf.at[1], r_buf.at[0], ssem.at[rnd, d, 1], rsem.at[rnd, d, 0],
                device_id=(hi,), device_id_type=pl.DeviceIdType.MESH,
            )
            c_lo = pltpu.make_async_remote_copy(
                s_buf.at[0], r_buf.at[1], ssem.at[rnd, d, 0], rsem.at[rnd, d, 1],
                device_id=(lo,), device_id_type=pl.DeviceIdType.MESH,
            )

            @pl.when(has_hi)
            def _():
                c_hi.start()

            @pl.when(has_lo)
            def _():
                c_lo.start()

            @pl.when(has_hi)
            def _():
                c_hi.wait_send()
                c_lo.wait_recv()
                fixup(7, r_buf.at[1])

            @pl.when(has_lo)
            def _():
                c_lo.wait_send()
                c_hi.wait_recv()
                fixup(0, r_buf.at[0])

        def fix_j(side, buf):
            for f in range(nf):
                x[f, :, side] = x[f, :, side] + buf[f]

        pair(sj, rj, 0, right, left, has_right, has_left, fix_j)

        for f in range(nf):
            si[0, f] = x[f, 0]
            si[1, f] = x[f, 7]

        def fix_i(side, buf):
            for f in range(nf):
                x[f, side] = x[f, side] + buf[f]

        pair(si, ri, 1, up, down, has_up, has_down, fix_i)

    def flow():
        return (vel_ref[0], vel_ref[1], vel_ref[2])

    x1[0] = mass_ref[...]

    def r1_body(f, c):
        x1[f + 1] = forward_terms(fld_ref[f], flow(), mass_ref[...], kap_ref[f], tab_ref)
        return c

    lax.fori_loop(0, 3, r1_body, 0)
    exchange(x1, 4, 0, sj1, rj1, si1, ri1)
    ms_ref[...] = x1[0]

    def f1_body(f, c):
        f1_ref[f] = fld_ref[f] + time_step * x1[f + 1] / ms_ref[...]
        x2[f + 3] = adj_ref[f] / ms_ref[...]
        return c

    lax.fori_loop(0, 3, f1_body, 0)

    def r2_body(f, c):
        x2[f] = forward_terms(f1_ref[f], flow(), mass_ref[...], kap_ref[f], tab_ref)
        return c

    lax.fori_loop(0, 3, r2_body, 0)
    exchange(x2, 6, 1, sj2, rj2, si2, ri2)

    def a1_body(f, c):
        out_f_ref[f] = f1_ref[f] + time_step * x2[f] / ms_ref[...]
        a1 = adj_ref[f] + time_step * adjoint_terms(x2[f + 3], flow(), mass_ref[...], kap_ref[f], tab_ref)
        a1_ref[f] = a1
        x3[f] = a1 / ms_ref[...]
        return c

    lax.fori_loop(0, 3, a1_body, 0)

    exchange(x3, 3, 2, sj3, rj3, si3, ri3)

    def a2_body(f, c):
        out_a_ref[f] = a1_ref[f] + time_step * adjoint_terms(x3[f], flow(), mass_ref[...], kap_ref[f], tab_ref)
        return c

    lax.fori_loop(0, 3, a2_body, 0)

    for f in range(3):
        out_f_in[f] = permute(out_f_ref[f].reshape(512, 128), pout_ref[...])
        out_a_in[f] = permute(out_a_ref[f].reshape(512, 128), pout_ref[...])


def fused(fields, adjoint, flow, mass, table, p_in, p_out, kappa, ndev, cols):
    cube = (8, 8, 8, 128)
    f32 = jnp.float32
    vmem = pl.BlockSpec(memory_space=pltpu.VMEM)
    smem = pl.BlockSpec(memory_space=pltpu.SMEM)
    scratch = [
        pltpu.VMEM((3,) + cube, f32),
        pltpu.VMEM((3,) + cube, f32),
        pltpu.VMEM((3,) + cube, f32),
        pltpu.VMEM(cube, f32),
        pltpu.VMEM((3,) + cube, f32),
        pltpu.VMEM((3,) + cube, f32),
        pltpu.VMEM((4,) + cube, f32),
        pltpu.VMEM((6,) + cube, f32),
        pltpu.VMEM((3,) + cube, f32),
        pltpu.VMEM(cube, f32),
        pltpu.VMEM((3,) + cube, f32),
        pltpu.VMEM((3,) + cube, f32),
    ]
    for nf in (4, 6, 3):
        for _ in range(4):
            scratch.append(pltpu.VMEM((2, nf, 8, 8, 128), f32))
    scratch += [pltpu.SemaphoreType.DMA((3, 2, 2)), pltpu.SemaphoreType.DMA((3, 2, 2))]
    shape = fields.shape
    return pl.pallas_call(
        functools.partial(kernel, ndev, cols),
        out_shape=(jax.ShapeDtypeStruct(shape, f32), jax.ShapeDtypeStruct(shape, f32)),
        in_specs=[vmem, vmem, vmem, vmem, vmem, vmem, vmem, smem],
        out_specs=(vmem, vmem),
        scratch_shapes=scratch,
        compiler_params=pltpu.CompilerParams(
            collective_id=0, has_side_effects=True, vmem_limit_bytes=60 * 1024 * 1024
        ),
    )(fields, adjoint, flow, mass, table, p_in, p_out, kappa)


def shards(moment_fields, adjoint_fields, velocity, mass_weights, diffusivity, numbering):
    height_count = numbering.shape[0]
    ndev = lax.axis_size("elem")
    cols = ndev // DA
    height = numbering % height_count
    slot_index = lax.iota(jnp.int32, height_count)
    p_in = (height[:, None] == slot_index[None, :]).astype(jnp.bfloat16)
    p_out = (slot_index[:, None] == height[None, :]).astype(jnp.bfloat16)
    weights = jnp.asarray(WEIGHTS)
    weight_cube = (weights[:, None, None] * weights[None, :, None] * weights[None, None, :]).reshape(512, 1)
    mass_cube = mass_weights * weight_cube
    table = jnp.asarray(shift_tables())
    return fused(moment_fields, adjoint_fields, velocity, mass_cube, table, p_in, p_out, diffusivity, ndev, cols)


def solution(mesh):
    in_specs = (
        P(None, None, "elem"),
        P(None, None, "elem"),
        P(None, None, "elem"),
        P(None, "elem"),
        P(),
        P("elem"),
    )
    out_specs = (P(None, None, "elem"), P(None, None, "elem"))
    return jax.shard_map(shards, mesh=mesh, in_specs=in_specs, out_specs=out_specs, check_vma=False)
```

```python
import functools

import jax
import jax.numpy as jnp
import numpy as np
from jax import lax
from jax.experimental import pallas as pl
from jax.experimental.pallas import tpu as pltpu
from jax.sharding import PartitionSpec as P

DA = 4

time_step = 0.001


def gll_tables():
    points = [
        -1.0,
        -0.8717401485096066,
        -0.5917001814331423,
        -0.2092992179024789,
        0.2092992179024789,
        0.5917001814331423,
        0.8717401485096066,
        1.0,
    ]
    weights = [
        0.03571428571428571,
        0.21070422714350603,
        0.3411226924835044,
        0.4124587946587038,
        0.4124587946587038,
        0.3411226924835044,
        0.21070422714350603,
        0.03571428571428571,
    ]
    barycentric = []
    for left_index in range(8):
        product = 1.0
        for right_index in range(8):
            if right_index != left_index:
                product = product * (points[left_index] - points[right_index])
        barycentric.append(1.0 / product)
    derivative = np.zeros((8, 8))
    for left_index in range(8):
        row_total = 0.0
        for right_index in range(8):
            if left_index != right_index:
                entry = (
                    barycentric[right_index]
                    / barycentric[left_index]
                    / (points[left_index] - points[right_index])
                )
                derivative[left_index, right_index] = entry
                row_total = row_total + entry
        derivative[left_index, left_index] = -row_total
    return derivative.astype(np.float32), np.asarray(weights, dtype=np.float32)


DM, WEIGHTS = gll_tables()
DMC = [[float(DM[p, q]) for q in range(8)] for p in range(8)]


def shift_tables():
    fwd = np.zeros((8, 8, 128), np.float32)
    bwd = np.zeros((8, 8, 128), np.float32)
    for s in range(8):
        for p in range(8):
            fwd[s, p, :] = DM[p, (p - s) % 8]
            bwd[s, p, :] = DM[(p - s) % 8, p]
    return np.concatenate([fwd, bwd], axis=0)


def along_major(v, axis, transpose):
    parts = []
    for p in range(8):
        acc = None
        for q in range(8):
            c = DMC[q][p] if transpose else DMC[p][q]
            term = c * (v[q] if axis == 0 else v[:, q])
            acc = term if acc is None else acc + term
        parts.append(acc)
    return jnp.stack(parts, axis=axis)


def along_sublane(v, tab_ref, base):
    acc = None
    for s in range(8):
        rolled = v if s == 0 else pltpu.roll(v, s, 2)
        term = tab_ref[base + s] * rolled
        acc = term if acc is None else acc + term
    return acc


def gradients(v, tab_ref):
    return (
        along_major(v, 0, False),
        along_major(v, 1, False),
        along_sublane(v, tab_ref, 0),
    )


def transposed(v, tab_ref, direction):
    if direction == 0:
        return along_major(v, 0, True)
    if direction == 1:
        return along_major(v, 1, True)
    return along_sublane(v, tab_ref, 8)


def forward_terms(q, flow, mass, kappa, tab_ref):
    g = gradients(q, tab_ref)
    advect = flow[0] * g[0] + flow[1] * g[1] + flow[2] * g[2]
    diffuse = transposed(mass * g[0], tab_ref, 0)
    diffuse = diffuse + transposed(mass * g[1], tab_ref, 1)
    diffuse = diffuse + transposed(mass * g[2], tab_ref, 2)
    return -(mass * advect) - kappa * diffuse


def adjoint_terms(q, flow, mass, kappa, tab_ref):
    g = gradients(q, tab_ref)
    summed = transposed(mass * (flow[0] * q + kappa * g[0]), tab_ref, 0)
    summed = summed + transposed(mass * (flow[1] * q + kappa * g[1]), tab_ref, 1)
    summed = summed + transposed(mass * (flow[2] * q + kappa * g[2]), tab_ref, 2)
    return -summed


def z_assemble(v):
    shape = v.shape
    sub = lax.broadcasted_iota(jnp.int32, shape, 2)
    lane = lax.broadcasted_iota(jnp.int32, shape, 3)
    below = pltpu.roll(pltpu.roll(v, 1, 2), 1, 3)
    above = pltpu.roll(pltpu.roll(v, 7, 2), 127, 3)
    zero = jnp.zeros_like(v)
    v = v + jnp.where((sub == 0) & (lane > 0), below, zero)
    return v + jnp.where((sub == 7) & (lane < 127), above, zero)


def permute(x, pm):
    bf = jnp.bfloat16
    f32 = jnp.float32
    x1 = x.astype(bf)
    r1 = x - x1.astype(f32)
    x2 = r1.astype(bf)
    x3 = (r1 - x2.astype(f32)).astype(bf)
    y = jnp.dot(x1, pm, preferred_element_type=f32)
    y = y + jnp.dot(x2, pm, preferred_element_type=f32)
    return y + jnp.dot(x3, pm, preferred_element_type=f32)


def kernel(
    ndev,
    cols,
    fld_in,
    adj_in,
    vel_in,
    mass_in,
    tab_ref,
    pin_ref,
    pout_ref,
    kap_ref,
    out_f_in,
    out_a_in,
    fld_ref,
    adj_ref,
    vel_ref,
    mass_ref,
    out_f_ref,
    out_a_ref,
    ms_ref,
    f1_ref,
    a1_ref,
    xs,
    sj,
    rj,
    si,
    ri,
    ssem,
    rsem,
):
    me = lax.axis_index("elem")
    column = (me + cols // 2) % ndev
    place = column % cols
    row = column // cols
    right = (me + 1) % ndev
    left = (me + ndev - 1) % ndev
    up = (me + cols) % ndev
    down = (me + ndev - cols) % ndev
    has_right = place < cols - 1
    has_left = place > 0
    has_up = row < DA - 1
    has_down = row > 0

    barrier = pltpu.get_barrier_semaphore()
    for nb in (left, right, up, down):
        pl.semaphore_signal(barrier, inc=1, device_id=(nb,), device_id_type=pl.DeviceIdType.MESH)
    pl.semaphore_wait(barrier, 4)

    def sort_in(src_ref, dst_ref):
        dst_ref[...] = permute(src_ref[...], pin_ref[...]).reshape(dst_ref.shape)

    for f in range(3):
        sort_in(fld_in.at[f], fld_ref.at[f])
        sort_in(adj_in.at[f], adj_ref.at[f])
        sort_in(vel_in.at[f], vel_ref.at[f])
    sort_in(mass_in, mass_ref)

    links = (
        (sj, rj, right, left, has_right, has_left),
        (si, ri, up, down, has_up, has_down),
    )

    def copies(u, d):
        s_buf, r_buf, hi, lo = links[d][:4]
        c_hi = pltpu.make_async_remote_copy(
            s_buf.at[u, 1], r_buf.at[u, 0], ssem.at[u, d, 1], rsem.at[u, d, 0],
            device_id=(hi,), device_id_type=pl.DeviceIdType.MESH,
        )
        c_lo = pltpu.make_async_remote_copy(
            s_buf.at[u, 0], r_buf.at[u, 1], ssem.at[u, d, 0], rsem.at[u, d, 1],
            device_id=(lo,), device_id_type=pl.DeviceIdType.MESH,
        )
        return c_hi, c_lo

    def face(u, d, side):
        return xs.at[u, :, side] if d == 0 else xs.at[u, side]

    def send(u, d):
        s_buf = links[d][0]
        s_buf[u, 0] = face(u, d, 0)[...]
        s_buf[u, 1] = face(u, d, 7)[...]
        c_hi, c_lo = copies(u, d)
        has_hi, has_lo = links[d][4:]

        @pl.when(has_hi)
        def _():
            c_hi.start()

        @pl.when(has_lo)
        def _():
            c_lo.start()

    def finish(u, d):
        r_buf = links[d][1]
        c_hi, c_lo = copies(u, d)
        has_hi, has_lo = links[d][4:]

        @pl.when(has_hi)
        def _():
            c_hi.wait_send()
            c_lo.wait_recv()
            top = face(u, d, 7)
            top[...] = top[...] + r_buf[u, 1]

        @pl.when(has_lo)
        def _():
            c_lo.wait_send()
            c_hi.wait_recv()
            bottom = face(u, d, 0)
            bottom[...] = bottom[...] + r_buf[u, 0]

    class Unit:
        def __init__(self, u, done):
            self.u = u
            self.stage = 0
            self.done = done
            xs[u] = z_assemble(xs[u])
            send(u, 0)

        def advance(self):
            finish(self.u, self.stage)
            if self.stage == 0:
                send(self.u, 1)
                self.stage = 1
                return False
            self.done()
            return True

    def flow():
        return (vel_ref[0], vel_ref[1], vel_ref[2])

    ready = []
    fresh = []
    state = {"ms": False}

    def mass_done():
        ms_ref[...] = xs[0]
        state["ms"] = True
        for f in range(3):
            xs[7 + f] = adj_ref[f] / ms_ref[...]
            fresh.append(Unit(7 + f, functools.partial(adjoint_first_done, f)))

    def forward_first(f):
        xs[1 + f] = forward_terms(fld_ref[f], flow(), mass_ref[...], kap_ref[f], tab_ref)
        fresh.append(Unit(1 + f, functools.partial(forward_first_done, f)))

    def forward_first_done(f):
        assert state["ms"]
        f1_ref[f] = fld_ref[f] + time_step * xs[1 + f] / ms_ref[...]
        ready.append(functools.partial(forward_second, f))

    def forward_second(f):
        xs[4 + f] = forward_terms(f1_ref[f], flow(), mass_ref[...], kap_ref[f], tab_ref)
        fresh.append(Unit(4 + f, functools.partial(forward_second_done, f)))

    def forward_second_done(f):
        out_f_ref[f] = f1_ref[f] + time_step * xs[4 + f] / ms_ref[...]

    def adjoint_first_done(f):
        ready.append(functools.partial(adjoint_second, f))

    def adjoint_second(f):
        a1 = adj_ref[f] + time_step * adjoint_terms(xs[7 + f], flow(), mass_ref[...], kap_ref[f], tab_ref)
        a1_ref[f] = a1
        xs[10 + f] = a1 / ms_ref[...]
        fresh.append(Unit(10 + f, functools.partial(adjoint_second_done, f)))

    def adjoint_second_done(f):
        ready.append(functools.partial(adjoint_third, f))

    def adjoint_third(f):
        out_a_ref[f] = a1_ref[f] + time_step * adjoint_terms(xs[10 + f], flow(), mass_ref[...], kap_ref[f], tab_ref)

    xs[0] = mass_ref[...]
    pending = [Unit(0, mass_done)]
    for f in range(3):
        ready.append(functools.partial(forward_first, f))
    while ready or pending or fresh:
        if ready:
            ready.pop(0)()
        for unit in list(pending):
            if unit.advance():
                pending.remove(unit)
        pending += fresh
        fresh.clear()

    for f in range(3):
        out_f_in[f] = permute(out_f_ref[f].reshape(512, 128), pout_ref[...])
        out_a_in[f] = permute(out_a_ref[f].reshape(512, 128), pout_ref[...])


def fused(fields, adjoint, flow, mass, table, p_in, p_out, kappa, ndev, cols):
    cube = (8, 8, 8, 128)
    f32 = jnp.float32
    units = 13
    vmem = pl.BlockSpec(memory_space=pltpu.VMEM)
    smem = pl.BlockSpec(memory_space=pltpu.SMEM)
    scratch = [
        pltpu.VMEM((3,) + cube, f32),
        pltpu.VMEM((3,) + cube, f32),
        pltpu.VMEM((3,) + cube, f32),
        pltpu.VMEM(cube, f32),
        pltpu.VMEM((3,) + cube, f32),
        pltpu.VMEM((3,) + cube, f32),
        pltpu.VMEM(cube, f32),
        pltpu.VMEM((3,) + cube, f32),
        pltpu.VMEM((3,) + cube, f32),
        pltpu.VMEM((units,) + cube, f32),
    ]
    for _ in range(4):
        scratch.append(pltpu.VMEM((units, 2, 8, 8, 128), f32))
    scratch += [pltpu.SemaphoreType.DMA((units, 2, 2)), pltpu.SemaphoreType.DMA((units, 2, 2))]
    shape = fields.shape
    return pl.pallas_call(
        functools.partial(kernel, ndev, cols),
        out_shape=(jax.ShapeDtypeStruct(shape, f32), jax.ShapeDtypeStruct(shape, f32)),
        in_specs=[vmem, vmem, vmem, vmem, vmem, vmem, vmem, smem],
        out_specs=(vmem, vmem),
        scratch_shapes=scratch,
        compiler_params=pltpu.CompilerParams(
            collective_id=0, has_side_effects=True, vmem_limit_bytes=60 * 1024 * 1024
        ),
    )(fields, adjoint, flow, mass, table, p_in, p_out, kappa)


def shards(moment_fields, adjoint_fields, velocity, mass_weights, diffusivity, numbering):
    height_count = numbering.shape[0]
    ndev = lax.axis_size("elem")
    cols = ndev // DA
    height = numbering % height_count
    slot_index = lax.iota(jnp.int32, height_count)
    p_in = (height[:, None] == slot_index[None, :]).astype(jnp.bfloat16)
    p_out = (slot_index[:, None] == height[None, :]).astype(jnp.bfloat16)
    weights = jnp.asarray(WEIGHTS)
    weight_cube = (weights[:, None, None] * weights[None, :, None] * weights[None, None, :]).reshape(512, 1)
    mass_cube = mass_weights * weight_cube
    table = jnp.asarray(shift_tables())
    return fused(moment_fields, adjoint_fields, velocity, mass_cube, table, p_in, p_out, diffusivity, ndev, cols)


def solution(mesh):
    in_specs = (
        P(None, None, "elem"),
        P(None, None, "elem"),
        P(None, None, "elem"),
        P(None, "elem"),
        P(),
        P("elem"),
    )
    out_specs = (P(None, None, "elem"), P(None, None, "elem"))
    return jax.shard_map(shards, mesh=mesh, in_specs=in_specs, out_specs=out_specs, check_vma=False)
```

```python
import functools

import jax
import jax.numpy as jnp
import numpy as np
from jax import lax
from jax.experimental import pallas as pl
from jax.experimental.pallas import tpu as pltpu
from jax.sharding import PartitionSpec as P

DA = 4

time_step = 0.001


def gll_tables():
    points = [
        -1.0,
        -0.8717401485096066,
        -0.5917001814331423,
        -0.2092992179024789,
        0.2092992179024789,
        0.5917001814331423,
        0.8717401485096066,
        1.0,
    ]
    weights = [
        0.03571428571428571,
        0.21070422714350603,
        0.3411226924835044,
        0.4124587946587038,
        0.4124587946587038,
        0.3411226924835044,
        0.21070422714350603,
        0.03571428571428571,
    ]
    barycentric = []
    for left_index in range(8):
        product = 1.0
        for right_index in range(8):
            if right_index != left_index:
                product = product * (points[left_index] - points[right_index])
        barycentric.append(1.0 / product)
    derivative = np.zeros((8, 8))
    for left_index in range(8):
        row_total = 0.0
        for right_index in range(8):
            if left_index != right_index:
                entry = (
                    barycentric[right_index]
                    / barycentric[left_index]
                    / (points[left_index] - points[right_index])
                )
                derivative[left_index, right_index] = entry
                row_total = row_total + entry
        derivative[left_index, left_index] = -row_total
    return derivative.astype(np.float32), np.asarray(weights, dtype=np.float32)


DM, WEIGHTS = gll_tables()
DMC = [[float(DM[p, q]) for q in range(8)] for p in range(8)]


def shift_tables():
    fwd = np.zeros((8, 8, 128), np.float32)
    bwd = np.zeros((8, 8, 128), np.float32)
    for s in range(8):
        for p in range(8):
            fwd[s, p, :] = DM[p, (p - s) % 8]
            bwd[s, p, :] = DM[(p - s) % 8, p]
    return np.concatenate([fwd, bwd], axis=0)


def along_major(v, axis, transpose):
    parts = []
    for p in range(8):
        acc = None
        for q in range(8):
            c = DMC[q][p] if transpose else DMC[p][q]
            term = c * (v[q] if axis == 0 else v[:, q])
            acc = term if acc is None else acc + term
        parts.append(acc)
    return jnp.stack(parts, axis=axis)


def along_sublane(v, tab_ref, base):
    acc = None
    for s in range(8):
        rolled = v if s == 0 else pltpu.roll(v, s, 2)
        term = tab_ref[base + s] * rolled
        acc = term if acc is None else acc + term
    return acc


def gradients(v, tab_ref):
    return (
        along_major(v, 0, False),
        along_major(v, 1, False),
        along_sublane(v, tab_ref, 0),
    )


def transposed(v, tab_ref, direction):
    if direction == 0:
        return along_major(v, 0, True)
    if direction == 1:
        return along_major(v, 1, True)
    return along_sublane(v, tab_ref, 8)


def forward_terms(q, flow, mass, kappa, tab_ref):
    g = gradients(q, tab_ref)
    advect = flow[0] * g[0] + flow[1] * g[1] + flow[2] * g[2]
    diffuse = transposed(mass * g[0], tab_ref, 0)
    diffuse = diffuse + transposed(mass * g[1], tab_ref, 1)
    diffuse = diffuse + transposed(mass * g[2], tab_ref, 2)
    return -(mass * advect) - kappa * diffuse


def adjoint_terms(q, flow, mass, kappa, tab_ref):
    g = gradients(q, tab_ref)
    summed = transposed(mass * (flow[0] * q + kappa * g[0]), tab_ref, 0)
    summed = summed + transposed(mass * (flow[1] * q + kappa * g[1]), tab_ref, 1)
    summed = summed + transposed(mass * (flow[2] * q + kappa * g[2]), tab_ref, 2)
    return -summed


def z_assemble(v):
    shape = v.shape
    sub = lax.broadcasted_iota(jnp.int32, shape, 2)
    lane = lax.broadcasted_iota(jnp.int32, shape, 3)
    below = pltpu.roll(pltpu.roll(v, 1, 2), 1, 3)
    above = pltpu.roll(pltpu.roll(v, 7, 2), 127, 3)
    zero = jnp.zeros_like(v)
    v = v + jnp.where((sub == 0) & (lane > 0), below, zero)
    return v + jnp.where((sub == 7) & (lane < 127), above, zero)


def permute(x, pm):
    bf = jnp.bfloat16
    f32 = jnp.float32
    x1 = x.astype(bf)
    r1 = x - x1.astype(f32)
    x2 = r1.astype(bf)
    x3 = (r1 - x2.astype(f32)).astype(bf)
    y = jnp.dot(x1, pm, preferred_element_type=f32)
    y = y + jnp.dot(x2, pm, preferred_element_type=f32)
    return y + jnp.dot(x3, pm, preferred_element_type=f32)


def kernel(
    ndev,
    cols,
    fld_in,
    adj_in,
    vel_in,
    mass_in,
    tab_ref,
    pin_ref,
    pout_ref,
    kap_ref,
    out_f_in,
    out_a_in,
    fld_ref,
    adj_ref,
    vel_ref,
    mass_ref,
    out_f_ref,
    out_a_ref,
    ms_ref,
    f1_ref,
    a1_ref,
    xs,
    sj,
    rj,
    si,
    ri,
    sd,
    rd,
    ssem,
    rsem,
):
    me = lax.axis_index("elem")
    column = (me + cols // 2) % ndev
    place = column % cols
    row = column // cols
    right = (me + 1) % ndev
    left = (me + ndev - 1) % ndev
    up = (me + cols) % ndev
    down = (me + ndev - cols) % ndev
    has_right = place < cols - 1
    has_left = place > 0
    has_up = row < DA - 1
    has_down = row > 0

    up_right = (me + cols + 1) % ndev
    up_left = (me + cols + ndev - 1) % ndev
    down_right = (me + 2 * ndev - cols + 1) % ndev
    down_left = (me + 2 * ndev - cols - 1) % ndev

    barrier = pltpu.get_barrier_semaphore()
    for nb in (left, right, up, down, up_right, up_left, down_right, down_left):
        pl.semaphore_signal(barrier, inc=1, device_id=(nb,), device_id_type=pl.DeviceIdType.MESH)
    pl.semaphore_wait(barrier, 8)

    def sort_in(src_ref, dst_ref):
        dst_ref[...] = permute(src_ref[...], pin_ref[...]).reshape(dst_ref.shape)

    for f in range(3):
        sort_in(fld_in.at[f], fld_ref.at[f])
        sort_in(adj_in.at[f], adj_ref.at[f])
        sort_in(vel_in.at[f], vel_ref.at[f])
    sort_in(mass_in, mass_ref)

    def plan(u):
        face_j = lambda side: xs.at[u, :, side]
        face_i = lambda side: xs.at[u, side]
        sends = [
            (sj.at[u, 1], rj.at[u, 0], right, has_right),
            (sj.at[u, 0], rj.at[u, 1], left, has_left),
            (si.at[u, 1], ri.at[u, 0], up, has_up),
            (si.at[u, 0], ri.at[u, 1], down, has_down),
            (sd.at[u, 0], rd.at[u, 0], up_right, has_up & has_right),
            (sd.at[u, 1], rd.at[u, 1], up_left, has_up & has_left),
            (sd.at[u, 2], rd.at[u, 2], down_right, has_down & has_right),
            (sd.at[u, 3], rd.at[u, 3], down_left, has_down & has_left),
        ]
        copies = [
            pltpu.make_async_remote_copy(
                s, d, ssem.at[u, k], rsem.at[u, k], device_id=(t,), device_id_type=pl.DeviceIdType.MESH
            )
            for k, (s, d, t, _) in enumerate(sends)
        ]
        recv_has = [has_left, has_right, has_down, has_up,
                    has_down & has_left, has_down & has_right, has_up & has_left, has_up & has_right]
        targets = [
            face_j(0), face_j(7), face_i(0), face_i(7),
            xs.at[u, 0, 0], xs.at[u, 0, 7], xs.at[u, 7, 0], xs.at[u, 7, 7],
        ]
        return sends, copies, recv_has, targets

    def start_unit(u):
        xs[u] = z_assemble(xs[u])
        sj[u, 0] = xs[u, :, 0]
        sj[u, 1] = xs[u, :, 7]
        si[u, 0] = xs[u, 0]
        si[u, 1] = xs[u, 7]
        sd[u, 0] = xs[u, 7, 7]
        sd[u, 1] = xs[u, 7, 0]
        sd[u, 2] = xs[u, 0, 7]
        sd[u, 3] = xs[u, 0, 0]
        sends, copies, _, _ = plan(u)
        for (_, _, _, has), c in zip(sends, copies):
            @pl.when(has)
            def _():
                c.start()

    def finish_unit(u):
        sends, copies, recv_has, targets = plan(u)
        for (_, _, _, has), c in zip(sends, copies):
            @pl.when(has)
            def _():
                c.wait_send()
        for k in range(8):
            @pl.when(recv_has[k])
            def _():
                copies[k].wait_recv()
                targets[k][...] = targets[k][...] + sends[k][1][...]

    def flow():
        return (vel_ref[0], vel_ref[1], vel_ref[2])

    def forward_first(f):
        xs[1 + f] = forward_terms(fld_ref[f], flow(), mass_ref[...], kap_ref[f], tab_ref)
        start_unit(1 + f)

    def forward_second(f):
        finish_unit(1 + f)
        f1 = fld_ref[f] + time_step * xs[1 + f] / ms_ref[...]
        f1_ref[f] = f1
        xs[4 + f] = forward_terms(f1, flow(), mass_ref[...], kap_ref[f], tab_ref)
        start_unit(4 + f)

    def adjoint_second(f):
        finish_unit(7 + f)
        a1 = adj_ref[f] + time_step * adjoint_terms(xs[7 + f], flow(), mass_ref[...], kap_ref[f], tab_ref)
        a1_ref[f] = a1
        xs[10 + f] = a1 / ms_ref[...]
        start_unit(10 + f)

    def adjoint_third(f):
        finish_unit(10 + f)
        out_a_ref[f] = a1_ref[f] + time_step * adjoint_terms(xs[10 + f], flow(), mass_ref[...], kap_ref[f], tab_ref)

    xs[0] = mass_ref[...]
    start_unit(0)
    forward_first(0)
    forward_first(1)
    finish_unit(0)
    ms_ref[...] = xs[0]
    for f in range(3):
        xs[7 + f] = adj_ref[f] / ms_ref[...]
        start_unit(7 + f)
    forward_first(2)
    for f in range(3):
        forward_second(f)
    for f in range(3):
        adjoint_second(f)
    for f in range(3):
        adjoint_third(f)
    for f in range(3):
        finish_unit(4 + f)
        out_f_ref[f] = f1_ref[f] + time_step * xs[4 + f] / ms_ref[...]

    for f in range(3):
        out_f_in[f] = permute(out_f_ref[f].reshape(512, 128), pout_ref[...])
        out_a_in[f] = permute(out_a_ref[f].reshape(512, 128), pout_ref[...])


def fused(fields, adjoint, flow, mass, table, p_in, p_out, kappa, ndev, cols):
    cube = (8, 8, 8, 128)
    f32 = jnp.float32
    units = 13
    vmem = pl.BlockSpec(memory_space=pltpu.VMEM)
    smem = pl.BlockSpec(memory_space=pltpu.SMEM)
    scratch = [
        pltpu.VMEM((3,) + cube, f32),
        pltpu.VMEM((3,) + cube, f32),
        pltpu.VMEM((3,) + cube, f32),
        pltpu.VMEM(cube, f32),
        pltpu.VMEM((3,) + cube, f32),
        pltpu.VMEM((3,) + cube, f32),
        pltpu.VMEM(cube, f32),
        pltpu.VMEM((3,) + cube, f32),
        pltpu.VMEM((3,) + cube, f32),
        pltpu.VMEM((units,) + cube, f32),
    ]
    for _ in range(4):
        scratch.append(pltpu.VMEM((units, 2, 8, 8, 128), f32))
    for _ in range(2):
        scratch.append(pltpu.VMEM((units, 4, 8, 128), f32))
    scratch += [pltpu.SemaphoreType.DMA((units, 8)), pltpu.SemaphoreType.DMA((units, 8))]
    shape = fields.shape
    return pl.pallas_call(
        functools.partial(kernel, ndev, cols),
        out_shape=(jax.ShapeDtypeStruct(shape, f32), jax.ShapeDtypeStruct(shape, f32)),
        in_specs=[vmem, vmem, vmem, vmem, vmem, vmem, vmem, smem],
        out_specs=(vmem, vmem),
        scratch_shapes=scratch,
        compiler_params=pltpu.CompilerParams(
            collective_id=0, has_side_effects=True, vmem_limit_bytes=60 * 1024 * 1024
        ),
    )(fields, adjoint, flow, mass, table, p_in, p_out, kappa)


def shards(moment_fields, adjoint_fields, velocity, mass_weights, diffusivity, numbering):
    height_count = numbering.shape[0]
    ndev = lax.axis_size("elem")
    cols = ndev // DA
    height = numbering % height_count
    slot_index = lax.iota(jnp.int32, height_count)
    p_in = (height[:, None] == slot_index[None, :]).astype(jnp.bfloat16)
    p_out = (slot_index[:, None] == height[None, :]).astype(jnp.bfloat16)
    weights = jnp.asarray(WEIGHTS)
    weight_cube = (weights[:, None, None] * weights[None, :, None] * weights[None, None, :]).reshape(512, 1)
    mass_cube = mass_weights * weight_cube
    table = jnp.asarray(shift_tables())
    return fused(moment_fields, adjoint_fields, velocity, mass_cube, table, p_in, p_out, diffusivity, ndev, cols)


def solution(mesh):
    in_specs = (
        P(None, None, "elem"),
        P(None, None, "elem"),
        P(None, None, "elem"),
        P(None, "elem"),
        P(),
        P("elem"),
    )
    out_specs = (P(None, None, "elem"), P(None, None, "elem"))
    return jax.shard_map(shards, mesh=mesh, in_specs=in_specs, out_specs=out_specs, check_vma=False)
```

```python
import functools

import jax
import jax.numpy as jnp
import numpy as np
from jax import lax
from jax.experimental import pallas as pl
from jax.experimental.pallas import tpu as pltpu
from jax.sharding import PartitionSpec as P

DA = 4

time_step = 0.001


def gll_tables():
    points = [
        -1.0,
        -0.8717401485096066,
        -0.5917001814331423,
        -0.2092992179024789,
        0.2092992179024789,
        0.5917001814331423,
        0.8717401485096066,
        1.0,
    ]
    weights = [
        0.03571428571428571,
        0.21070422714350603,
        0.3411226924835044,
        0.4124587946587038,
        0.4124587946587038,
        0.3411226924835044,
        0.21070422714350603,
        0.03571428571428571,
    ]
    barycentric = []
    for left_index in range(8):
        product = 1.0
        for right_index in range(8):
            if right_index != left_index:
                product = product * (points[left_index] - points[right_index])
        barycentric.append(1.0 / product)
    derivative = np.zeros((8, 8))
    for left_index in range(8):
        row_total = 0.0
        for right_index in range(8):
            if left_index != right_index:
                entry = (
                    barycentric[right_index]
                    / barycentric[left_index]
                    / (points[left_index] - points[right_index])
                )
                derivative[left_index, right_index] = entry
                row_total = row_total + entry
        derivative[left_index, left_index] = -row_total
    return derivative.astype(np.float32), np.asarray(weights, dtype=np.float32)


DM, WEIGHTS = gll_tables()
DMC = [[float(DM[p, q]) for q in range(8)] for p in range(8)]


def shift_tables():
    fwd = np.zeros((8, 8, 128), np.float32)
    bwd = np.zeros((8, 8, 128), np.float32)
    for s in range(8):
        for p in range(8):
            fwd[s, p, :] = DM[p, (p - s) % 8]
            bwd[s, p, :] = DM[(p - s) % 8, p]
    return np.concatenate([fwd, bwd], axis=0)


def along_major(v, axis, transpose):
    parts = []
    for p in range(8):
        acc = None
        for q in range(8):
            c = DMC[q][p] if transpose else DMC[p][q]
            term = c * (v[q] if axis == 0 else v[:, q])
            acc = term if acc is None else acc + term
        parts.append(acc)
    return jnp.stack(parts, axis=axis)


def along_sublane(v, tab_ref, base):
    acc = None
    for s in range(8):
        rolled = v if s == 0 else pltpu.roll(v, s, 2)
        term = tab_ref[base + s] * rolled
        acc = term if acc is None else acc + term
    return acc


def gradients(v, tab_ref):
    return (
        along_major(v, 0, False),
        along_major(v, 1, False),
        along_sublane(v, tab_ref, 0),
    )


def transposed(v, tab_ref, direction):
    if direction == 0:
        return along_major(v, 0, True)
    if direction == 1:
        return along_major(v, 1, True)
    return along_sublane(v, tab_ref, 8)


def forward_terms(q, flow, mass, kappa, tab_ref):
    g = gradients(q, tab_ref)
    advect = flow[0] * g[0] + flow[1] * g[1] + flow[2] * g[2]
    diffuse = transposed(mass * g[0], tab_ref, 0)
    diffuse = diffuse + transposed(mass * g[1], tab_ref, 1)
    diffuse = diffuse + transposed(mass * g[2], tab_ref, 2)
    return -(mass * advect) - kappa * diffuse


def adjoint_terms(q, flow, mass, kappa, tab_ref):
    g = gradients(q, tab_ref)
    summed = transposed(mass * (flow[0] * q + kappa * g[0]), tab_ref, 0)
    summed = summed + transposed(mass * (flow[1] * q + kappa * g[1]), tab_ref, 1)
    summed = summed + transposed(mass * (flow[2] * q + kappa * g[2]), tab_ref, 2)
    return -summed


def z_assemble(v):
    shape = v.shape
    sub = lax.broadcasted_iota(jnp.int32, shape, 2)
    lane = lax.broadcasted_iota(jnp.int32, shape, 3)
    below = pltpu.roll(pltpu.roll(v, 1, 2), 1, 3)
    above = pltpu.roll(pltpu.roll(v, 7, 2), 127, 3)
    zero = jnp.zeros_like(v)
    v = v + jnp.where((sub == 0) & (lane > 0), below, zero)
    return v + jnp.where((sub == 7) & (lane < 127), above, zero)


def permute(x, pm):
    bf = jnp.bfloat16
    f32 = jnp.float32
    x1 = x.astype(bf)
    r1 = x - x1.astype(f32)
    x2 = r1.astype(bf)
    x3 = (r1 - x2.astype(f32)).astype(bf)
    y = jnp.dot(x1, pm, preferred_element_type=f32)
    y = y + jnp.dot(x2, pm, preferred_element_type=f32)
    return y + jnp.dot(x3, pm, preferred_element_type=f32)


def kernel(
    ndev,
    cols,
    fld_in,
    adj_in,
    vel_in,
    mass_in,
    tab_ref,
    pin_ref,
    pout_ref,
    kap_ref,
    out_f_in,
    out_a_in,
    fld_ref,
    adj_ref,
    vel_ref,
    mass_ref,
    out_f_ref,
    out_a_ref,
    ms_ref,
    f1_ref,
    a1_ref,
    xs,
    sj,
    rj,
    si,
    ri,
    sd,
    rd,
    ssem,
    rsem,
):
    me = lax.axis_index("elem")
    column = (me + cols // 2) % ndev
    place = column % cols
    row = column // cols
    right = (me + 1) % ndev
    left = (me + ndev - 1) % ndev
    up = (me + cols) % ndev
    down = (me + ndev - cols) % ndev
    has_right = place < cols - 1
    has_left = place > 0
    has_up = row < DA - 1
    has_down = row > 0

    up_right = (me + cols + 1) % ndev
    up_left = (me + cols + ndev - 1) % ndev
    down_right = (me + 2 * ndev - cols + 1) % ndev
    down_left = (me + 2 * ndev - cols - 1) % ndev

    barrier = pltpu.get_barrier_semaphore()
    for nb in (left, right, up, down, up_right, up_left, down_right, down_left):
        pl.semaphore_signal(barrier, inc=1, device_id=(nb,), device_id_type=pl.DeviceIdType.MESH)
    pl.semaphore_wait(barrier, 8)

    def sort_in(src_ref, dst_ref):
        dst_ref[...] = permute(src_ref[...], pin_ref[...]).reshape(dst_ref.shape)

    for f in range(3):
        sort_in(fld_in.at[f], fld_ref.at[f])
        sort_in(adj_in.at[f], adj_ref.at[f])
        sort_in(vel_in.at[f], vel_ref.at[f])
    sort_in(mass_in, mass_ref)

    groups = ((0, 1), (1, 4), (4, 7), (7, 10), (10, 13))

    def plan(g):
        lo, hi = groups[g]
        n = hi - lo
        sends = [
            (sj.at[g, 1, 0:n], rj.at[g, 0, 0:n], right, has_right),
            (sj.at[g, 0, 0:n], rj.at[g, 1, 0:n], left, has_left),
            (si.at[g, 1, 0:n], ri.at[g, 0, 0:n], up, has_up),
            (si.at[g, 0, 0:n], ri.at[g, 1, 0:n], down, has_down),
            (sd.at[g, 0, 0:n], rd.at[g, 0, 0:n], up_right, has_up & has_right),
            (sd.at[g, 1, 0:n], rd.at[g, 1, 0:n], up_left, has_up & has_left),
            (sd.at[g, 2, 0:n], rd.at[g, 2, 0:n], down_right, has_down & has_right),
            (sd.at[g, 3, 0:n], rd.at[g, 3, 0:n], down_left, has_down & has_left),
        ]
        copies = [
            pltpu.make_async_remote_copy(
                s, d, ssem.at[g, k], rsem.at[g, k], device_id=(t,), device_id_type=pl.DeviceIdType.MESH
            )
            for k, (s, d, t, _) in enumerate(sends)
        ]
        recv_has = [has_left, has_right, has_down, has_up,
                    has_down & has_left, has_down & has_right, has_up & has_left, has_up & has_right]
        targets = [
            xs.at[lo:hi, :, 0], xs.at[lo:hi, :, 7], xs.at[lo:hi, 0], xs.at[lo:hi, 7],
            xs.at[lo:hi, 0, 0], xs.at[lo:hi, 0, 7], xs.at[lo:hi, 7, 0], xs.at[lo:hi, 7, 7],
        ]
        return sends, copies, recv_has, targets

    def start_group(g):
        lo, hi = groups[g]
        n = hi - lo
        for u in range(lo, hi):
            xs[u] = z_assemble(xs[u])
        sj[g, 0, 0:n] = xs[lo:hi, :, 0]
        sj[g, 1, 0:n] = xs[lo:hi, :, 7]
        si[g, 0, 0:n] = xs[lo:hi, 0]
        si[g, 1, 0:n] = xs[lo:hi, 7]
        sd[g, 0, 0:n] = xs[lo:hi, 7, 7]
        sd[g, 1, 0:n] = xs[lo:hi, 7, 0]
        sd[g, 2, 0:n] = xs[lo:hi, 0, 7]
        sd[g, 3, 0:n] = xs[lo:hi, 0, 0]
        sends, copies, _, _ = plan(g)
        for (_, _, _, has), c in zip(sends, copies):
            @pl.when(has)
            def _():
                c.start()

    def finish_group(g):
        sends, copies, recv_has, targets = plan(g)
        for (_, _, _, has), c in zip(sends, copies):
            @pl.when(has)
            def _():
                c.wait_send()
        for k in range(8):
            @pl.when(recv_has[k])
            def _():
                copies[k].wait_recv()
                targets[k][...] = targets[k][...] + sends[k][1][...]

    def flow():
        return (vel_ref[0], vel_ref[1], vel_ref[2])

    xs[0] = mass_ref[...]
    start_group(0)
    xs[1] = forward_terms(fld_ref[0], flow(), mass_ref[...], kap_ref[0], tab_ref)
    finish_group(0)
    ms_ref[...] = xs[0]
    for f in range(3):
        xs[7 + f] = adj_ref[f] / ms_ref[...]
    start_group(3)
    for f in range(1, 3):
        xs[1 + f] = forward_terms(fld_ref[f], flow(), mass_ref[...], kap_ref[f], tab_ref)
    start_group(1)
    finish_group(3)
    for f in range(3):
        a1 = adj_ref[f] + time_step * adjoint_terms(xs[7 + f], flow(), mass_ref[...], kap_ref[f], tab_ref)
        a1_ref[f] = a1
        xs[10 + f] = a1 / ms_ref[...]
    start_group(4)
    finish_group(1)
    for f in range(3):
        f1 = fld_ref[f] + time_step * xs[1 + f] / ms_ref[...]
        f1_ref[f] = f1
        xs[4 + f] = forward_terms(f1, flow(), mass_ref[...], kap_ref[f], tab_ref)
    start_group(2)
    finish_group(4)
    for f in range(3):
        out_a_ref[f] = a1_ref[f] + time_step * adjoint_terms(xs[10 + f], flow(), mass_ref[...], kap_ref[f], tab_ref)
    finish_group(2)
    for f in range(3):
        out_f_ref[f] = f1_ref[f] + time_step * xs[4 + f] / ms_ref[...]

    for f in range(3):
        out_f_in[f] = permute(out_f_ref[f].reshape(512, 128), pout_ref[...])
        out_a_in[f] = permute(out_a_ref[f].reshape(512, 128), pout_ref[...])


def fused(fields, adjoint, flow, mass, table, p_in, p_out, kappa, ndev, cols):
    cube = (8, 8, 8, 128)
    f32 = jnp.float32
    units = 13
    vmem = pl.BlockSpec(memory_space=pltpu.VMEM)
    smem = pl.BlockSpec(memory_space=pltpu.SMEM)
    scratch = [
        pltpu.VMEM((3,) + cube, f32),
        pltpu.VMEM((3,) + cube, f32),
        pltpu.VMEM((3,) + cube, f32),
        pltpu.VMEM(cube, f32),
        pltpu.VMEM((3,) + cube, f32),
        pltpu.VMEM((3,) + cube, f32),
        pltpu.VMEM(cube, f32),
        pltpu.VMEM((3,) + cube, f32),
        pltpu.VMEM((3,) + cube, f32),
        pltpu.VMEM((units,) + cube, f32),
    ]
    groups = 5
    for _ in range(4):
        scratch.append(pltpu.VMEM((groups, 2, 3, 8, 8, 128), f32))
    for _ in range(2):
        scratch.append(pltpu.VMEM((groups, 4, 3, 8, 128), f32))
    scratch += [pltpu.SemaphoreType.DMA((groups, 8)), pltpu.SemaphoreType.DMA((groups, 8))]
    shape = fields.shape
    return pl.pallas_call(
        functools.partial(kernel, ndev, cols),
        out_shape=(jax.ShapeDtypeStruct(shape, f32), jax.ShapeDtypeStruct(shape, f32)),
        in_specs=[vmem, vmem, vmem, vmem, vmem, vmem, vmem, smem],
        out_specs=(vmem, vmem),
        scratch_shapes=scratch,
        compiler_params=pltpu.CompilerParams(
            collective_id=0, has_side_effects=True, vmem_limit_bytes=60 * 1024 * 1024
        ),
    )(fields, adjoint, flow, mass, table, p_in, p_out, kappa)


def shards(moment_fields, adjoint_fields, velocity, mass_weights, diffusivity, numbering):
    height_count = numbering.shape[0]
    ndev = lax.axis_size("elem")
    cols = ndev // DA
    height = numbering % height_count
    slot_index = lax.iota(jnp.int32, height_count)
    p_in = (height[:, None] == slot_index[None, :]).astype(jnp.bfloat16)
    p_out = (slot_index[:, None] == height[None, :]).astype(jnp.bfloat16)
    weights = jnp.asarray(WEIGHTS)
    weight_cube = (weights[:, None, None] * weights[None, :, None] * weights[None, None, :]).reshape(512, 1)
    mass_cube = mass_weights * weight_cube
    table = jnp.asarray(shift_tables())
    return fused(moment_fields, adjoint_fields, velocity, mass_cube, table, p_in, p_out, diffusivity, ndev, cols)


def solution(mesh):
    in_specs = (
        P(None, None, "elem"),
        P(None, None, "elem"),
        P(None, None, "elem"),
        P(None, "elem"),
        P(),
        P("elem"),
    )
    out_specs = (P(None, None, "elem"), P(None, None, "elem"))
    return jax.shard_map(shards, mesh=mesh, in_specs=in_specs, out_specs=out_specs, check_vma=False)
```

```python
import functools

import jax
import jax.numpy as jnp
import numpy as np
from jax import lax
from jax.experimental import pallas as pl
from jax.experimental.pallas import tpu as pltpu
from jax.sharding import PartitionSpec as P

DA = 4

time_step = 0.001


def gll_tables():
    points = [
        -1.0,
        -0.8717401485096066,
        -0.5917001814331423,
        -0.2092992179024789,
        0.2092992179024789,
        0.5917001814331423,
        0.8717401485096066,
        1.0,
    ]
    weights = [
        0.03571428571428571,
        0.21070422714350603,
        0.3411226924835044,
        0.4124587946587038,
        0.4124587946587038,
        0.3411226924835044,
        0.21070422714350603,
        0.03571428571428571,
    ]
    barycentric = []
    for left_index in range(8):
        product = 1.0
        for right_index in range(8):
            if right_index != left_index:
                product = product * (points[left_index] - points[right_index])
        barycentric.append(1.0 / product)
    derivative = np.zeros((8, 8))
    for left_index in range(8):
        row_total = 0.0
        for right_index in range(8):
            if left_index != right_index:
                entry = (
                    barycentric[right_index]
                    / barycentric[left_index]
                    / (points[left_index] - points[right_index])
                )
                derivative[left_index, right_index] = entry
                row_total = row_total + entry
        derivative[left_index, left_index] = -row_total
    return derivative.astype(np.float32), np.asarray(weights, dtype=np.float32)


DM, WEIGHTS = gll_tables()
DMC = [[float(DM[p, q]) for q in range(8)] for p in range(8)]


def shift_tables():
    fwd = np.zeros((8, 8, 128), np.float32)
    bwd = np.zeros((8, 8, 128), np.float32)
    for s in range(8):
        for p in range(8):
            fwd[s, p, :] = DM[p, (p - s) % 8]
            bwd[s, p, :] = DM[(p - s) % 8, p]
    return np.concatenate([fwd, bwd], axis=0)


def along_major(v, axis, transpose):
    parts = []
    for p in range(8):
        acc = None
        for q in range(8):
            c = DMC[q][p] if transpose else DMC[p][q]
            term = c * (v[q] if axis == 0 else v[:, q])
            acc = term if acc is None else acc + term
        parts.append(acc)
    return jnp.stack(parts, axis=axis)


def along_sublane(v, tab_ref, base):
    acc = None
    for s in range(8):
        rolled = v if s == 0 else pltpu.roll(v, s, 2)
        term = tab_ref[base + s] * rolled
        acc = term if acc is None else acc + term
    return acc


def gradients(v, tab_ref):
    return (
        along_major(v, 0, False),
        along_major(v, 1, False),
        along_sublane(v, tab_ref, 0),
    )


def transposed(v, tab_ref, direction):
    if direction == 0:
        return along_major(v, 0, True)
    if direction == 1:
        return along_major(v, 1, True)
    return along_sublane(v, tab_ref, 8)


def forward_terms(q, flow, mass, kappa, tab_ref):
    g = gradients(q, tab_ref)
    advect = flow[0] * g[0] + flow[1] * g[1] + flow[2] * g[2]
    diffuse = transposed(mass * g[0], tab_ref, 0)
    diffuse = diffuse + transposed(mass * g[1], tab_ref, 1)
    diffuse = diffuse + transposed(mass * g[2], tab_ref, 2)
    return -(mass * advect) - kappa * diffuse


def adjoint_terms(q, flow, mass, kappa, tab_ref):
    g = gradients(q, tab_ref)
    summed = transposed(mass * (flow[0] * q + kappa * g[0]), tab_ref, 0)
    summed = summed + transposed(mass * (flow[1] * q + kappa * g[1]), tab_ref, 1)
    summed = summed + transposed(mass * (flow[2] * q + kappa * g[2]), tab_ref, 2)
    return -summed


def z_assemble(v):
    shape = v.shape
    sub = lax.broadcasted_iota(jnp.int32, shape, 2)
    lane = lax.broadcasted_iota(jnp.int32, shape, 3)
    below = pltpu.roll(pltpu.roll(v, 1, 2), 1, 3)
    above = pltpu.roll(pltpu.roll(v, 7, 2), 127, 3)
    zero = jnp.zeros_like(v)
    v = v + jnp.where((sub == 0) & (lane > 0), below, zero)
    return v + jnp.where((sub == 7) & (lane < 127), above, zero)


def permute(x, pm):
    bf = jnp.bfloat16
    f32 = jnp.float32
    x1 = x.astype(bf)
    r1 = x - x1.astype(f32)
    x2 = r1.astype(bf)
    x3 = (r1 - x2.astype(f32)).astype(bf)
    y = jnp.dot(x1, pm, preferred_element_type=f32)
    y = y + jnp.dot(x2, pm, preferred_element_type=f32)
    return y + jnp.dot(x3, pm, preferred_element_type=f32)


def kernel(
    ndev,
    cols,
    fld_in,
    adj_in,
    vel_in,
    mass_in,
    tab_ref,
    pin_ref,
    pout_ref,
    kap_ref,
    out_f_in,
    out_a_in,
    fld_ref,
    adj_ref,
    vel_ref,
    mass_ref,
    out_f_ref,
    out_a_ref,
    ms_ref,
    f1_ref,
    a1_ref,
    xs,
    sj,
    rj,
    si,
    ri,
    sd,
    rd,
    ssem,
    rsem,
):
    me = lax.axis_index("elem")
    column = (me + cols // 2) % ndev
    place = column % cols
    row = column // cols
    right = (me + 1) % ndev
    left = (me + ndev - 1) % ndev
    up = (me + cols) % ndev
    down = (me + ndev - cols) % ndev
    has_right = place < cols - 1
    has_left = place > 0
    has_up = row < DA - 1
    has_down = row > 0

    up_right = (me + cols + 1) % ndev
    up_left = (me + cols + ndev - 1) % ndev
    down_right = (me + 2 * ndev - cols + 1) % ndev
    down_left = (me + 2 * ndev - cols - 1) % ndev

    barrier = pltpu.get_barrier_semaphore()
    for nb in (left, right, up, down, up_right, up_left, down_right, down_left):
        pl.semaphore_signal(barrier, inc=1, device_id=(nb,), device_id_type=pl.DeviceIdType.MESH)
    pl.semaphore_wait(barrier, 8)

    def sort_in(src_ref, dst_ref):
        dst_ref[...] = permute(src_ref[...], pin_ref[...]).reshape(dst_ref.shape)

    for f in range(3):
        sort_in(fld_in.at[f], fld_ref.at[f])
        sort_in(adj_in.at[f], adj_ref.at[f])
        sort_in(vel_in.at[f], vel_ref.at[f])
    sort_in(mass_in, mass_ref)

    groups = ((0, 4), (4, 7), (7, 10), (10, 13))

    def plan(g):
        lo, hi = groups[g]
        n = hi - lo
        sends = [
            (sj.at[g, 1, 0:n], rj.at[g, 0, 0:n], right, has_right),
            (sj.at[g, 0, 0:n], rj.at[g, 1, 0:n], left, has_left),
            (si.at[g, 1, 0:n], ri.at[g, 0, 0:n], up, has_up),
            (si.at[g, 0, 0:n], ri.at[g, 1, 0:n], down, has_down),
            (sd.at[g, 0, 0:n], rd.at[g, 0, 0:n], up_right, has_up & has_right),
            (sd.at[g, 1, 0:n], rd.at[g, 1, 0:n], up_left, has_up & has_left),
            (sd.at[g, 2, 0:n], rd.at[g, 2, 0:n], down_right, has_down & has_right),
            (sd.at[g, 3, 0:n], rd.at[g, 3, 0:n], down_left, has_down & has_left),
        ]
        copies = [
            pltpu.make_async_remote_copy(
                s, d, ssem.at[g, k], rsem.at[g, k], device_id=(t,), device_id_type=pl.DeviceIdType.MESH
            )
            for k, (s, d, t, _) in enumerate(sends)
        ]
        recv_has = [has_left, has_right, has_down, has_up,
                    has_down & has_left, has_down & has_right, has_up & has_left, has_up & has_right]
        targets = [
            xs.at[lo:hi, :, 0], xs.at[lo:hi, :, 7], xs.at[lo:hi, 0], xs.at[lo:hi, 7],
            xs.at[lo:hi, 0, 0], xs.at[lo:hi, 0, 7], xs.at[lo:hi, 7, 0], xs.at[lo:hi, 7, 7],
        ]
        return sends, copies, recv_has, targets

    def start_group(g):
        lo, hi = groups[g]
        n = hi - lo
        for u in range(lo, hi):
            xs[u] = z_assemble(xs[u])
        sj[g, 0, 0:n] = xs[lo:hi, :, 0]
        sj[g, 1, 0:n] = xs[lo:hi, :, 7]
        si[g, 0, 0:n] = xs[lo:hi, 0]
        si[g, 1, 0:n] = xs[lo:hi, 7]
        sd[g, 0, 0:n] = xs[lo:hi, 7, 7]
        sd[g, 1, 0:n] = xs[lo:hi, 7, 0]
        sd[g, 2, 0:n] = xs[lo:hi, 0, 7]
        sd[g, 3, 0:n] = xs[lo:hi, 0, 0]
        sends, copies, _, _ = plan(g)
        for (_, _, _, has), c in zip(sends, copies):
            @pl.when(has)
            def _():
                c.start()

    def finish_group(g):
        sends, copies, recv_has, targets = plan(g)
        for (_, _, _, has), c in zip(sends, copies):
            @pl.when(has)
            def _():
                c.wait_send()
        for k in range(8):
            @pl.when(recv_has[k])
            def _():
                copies[k].wait_recv()
                targets[k][...] = targets[k][...] + sends[k][1][...]

    def flow():
        return (vel_ref[0], vel_ref[1], vel_ref[2])

    xs[0] = mass_ref[...]
    for f in range(3):
        xs[1 + f] = adj_ref[f]
    start_group(0)
    for f in range(3):
        xs[4 + f] = forward_terms(fld_ref[f], flow(), mass_ref[...], kap_ref[f], tab_ref)
    start_group(1)
    finish_group(0)
    ms_ref[...] = xs[0]
    for f in range(3):
        gathered = xs[1 + f] / ms_ref[...]
        a1 = adj_ref[f] + time_step * adjoint_terms(gathered, flow(), mass_ref[...], kap_ref[f], tab_ref)
        a1_ref[f] = a1
        xs[7 + f] = a1 / ms_ref[...]
    start_group(2)
    finish_group(1)
    for f in range(3):
        f1 = fld_ref[f] + time_step * xs[4 + f] / ms_ref[...]
        f1_ref[f] = f1
        xs[10 + f] = forward_terms(f1, flow(), mass_ref[...], kap_ref[f], tab_ref)
    start_group(3)
    finish_group(2)
    for f in range(3):
        out_a_ref[f] = a1_ref[f] + time_step * adjoint_terms(xs[7 + f], flow(), mass_ref[...], kap_ref[f], tab_ref)
    finish_group(3)
    for f in range(3):
        out_f_ref[f] = f1_ref[f] + time_step * xs[10 + f] / ms_ref[...]

    for f in range(3):
        out_f_in[f] = permute(out_f_ref[f].reshape(512, 128), pout_ref[...])
        out_a_in[f] = permute(out_a_ref[f].reshape(512, 128), pout_ref[...])


def fused(fields, adjoint, flow, mass, table, p_in, p_out, kappa, ndev, cols):
    cube = (8, 8, 8, 128)
    f32 = jnp.float32
    units = 13
    vmem = pl.BlockSpec(memory_space=pltpu.VMEM)
    smem = pl.BlockSpec(memory_space=pltpu.SMEM)
    scratch = [
        pltpu.VMEM((3,) + cube, f32),
        pltpu.VMEM((3,) + cube, f32),
        pltpu.VMEM((3,) + cube, f32),
        pltpu.VMEM(cube, f32),
        pltpu.VMEM((3,) + cube, f32),
        pltpu.VMEM((3,) + cube, f32),
        pltpu.VMEM(cube, f32),
        pltpu.VMEM((3,) + cube, f32),
        pltpu.VMEM((3,) + cube, f32),
        pltpu.VMEM((units,) + cube, f32),
    ]
    groups = 4
    for _ in range(4):
        scratch.append(pltpu.VMEM((groups, 2, 4, 8, 8, 128), f32))
    for _ in range(2):
        scratch.append(pltpu.VMEM((groups, 4, 4, 8, 128), f32))
    scratch += [pltpu.SemaphoreType.DMA((groups, 8)), pltpu.SemaphoreType.DMA((groups, 8))]
    shape = fields.shape
    return pl.pallas_call(
        functools.partial(kernel, ndev, cols),
        out_shape=(jax.ShapeDtypeStruct(shape, f32), jax.ShapeDtypeStruct(shape, f32)),
        in_specs=[vmem, vmem, vmem, vmem, vmem, vmem, vmem, smem],
        out_specs=(vmem, vmem),
        scratch_shapes=scratch,
        compiler_params=pltpu.CompilerParams(
            collective_id=0, has_side_effects=True, vmem_limit_bytes=60 * 1024 * 1024
        ),
    )(fields, adjoint, flow, mass, table, p_in, p_out, kappa)


def shards(moment_fields, adjoint_fields, velocity, mass_weights, diffusivity, numbering):
    height_count = numbering.shape[0]
    ndev = lax.axis_size("elem")
    cols = ndev // DA
    height = numbering % height_count
    slot_index = lax.iota(jnp.int32, height_count)
    p_in = (height[:, None] == slot_index[None, :]).astype(jnp.bfloat16)
    p_out = (slot_index[:, None] == height[None, :]).astype(jnp.bfloat16)
    weights = jnp.asarray(WEIGHTS)
    weight_cube = (weights[:, None, None] * weights[None, :, None] * weights[None, None, :]).reshape(512, 1)
    mass_cube = mass_weights * weight_cube
    table = jnp.asarray(shift_tables())
    return fused(moment_fields, adjoint_fields, velocity, mass_cube, table, p_in, p_out, diffusivity, ndev, cols)


def solution(mesh):
    in_specs = (
        P(None, None, "elem"),
        P(None, None, "elem"),
        P(None, None, "elem"),
        P(None, "elem"),
        P(),
        P("elem"),
    )
    out_specs = (P(None, None, "elem"), P(None, None, "elem"))
    return jax.shard_map(shards, mesh=mesh, in_specs=in_specs, out_specs=out_specs, check_vma=False)
```

```python
import functools

import jax
import jax.numpy as jnp
import numpy as np
from jax import lax
from jax.experimental import pallas as pl
from jax.experimental.pallas import tpu as pltpu
from jax.sharding import PartitionSpec as P

DA = 4

time_step = 0.001


def gll_tables():
    points = [
        -1.0,
        -0.8717401485096066,
        -0.5917001814331423,
        -0.2092992179024789,
        0.2092992179024789,
        0.5917001814331423,
        0.8717401485096066,
        1.0,
    ]
    weights = [
        0.03571428571428571,
        0.21070422714350603,
        0.3411226924835044,
        0.4124587946587038,
        0.4124587946587038,
        0.3411226924835044,
        0.21070422714350603,
        0.03571428571428571,
    ]
    barycentric = []
    for left_index in range(8):
        product = 1.0
        for right_index in range(8):
            if right_index != left_index:
                product = product * (points[left_index] - points[right_index])
        barycentric.append(1.0 / product)
    derivative = np.zeros((8, 8))
    for left_index in range(8):
        row_total = 0.0
        for right_index in range(8):
            if left_index != right_index:
                entry = (
                    barycentric[right_index]
                    / barycentric[left_index]
                    / (points[left_index] - points[right_index])
                )
                derivative[left_index, right_index] = entry
                row_total = row_total + entry
        derivative[left_index, left_index] = -row_total
    return derivative.astype(np.float32), np.asarray(weights, dtype=np.float32)


DM, WEIGHTS = gll_tables()
DMC = [[float(DM[p, q]) for q in range(8)] for p in range(8)]


def shift_tables():
    fwd = np.zeros((8, 8, 128), np.float32)
    bwd = np.zeros((8, 8, 128), np.float32)
    for s in range(8):
        for p in range(8):
            fwd[s, p, :] = DM[p, (p - s) % 8]
            bwd[s, p, :] = DM[(p - s) % 8, p]
    cube = (WEIGHTS[:, None, None] * WEIGHTS[None, :, None]) * WEIGHTS[None, None, :]
    wrows = np.broadcast_to(cube.reshape(64, 8, 1), (64, 8, 128)).astype(np.float32)
    return np.concatenate([fwd, bwd, wrows], axis=0)


def along_major(v, axis, transpose):
    parts = []
    for p in range(8):
        acc = None
        for q in range(8):
            c = DMC[q][p] if transpose else DMC[p][q]
            term = c * (v[q] if axis == 0 else v[:, q])
            acc = term if acc is None else acc + term
        parts.append(acc)
    return jnp.stack(parts, axis=axis)


def along_sublane(v, tab_ref, base):
    acc = None
    for s in range(8):
        rolled = v if s == 0 else pltpu.roll(v, s, 2)
        term = tab_ref[base + s] * rolled
        acc = term if acc is None else acc + term
    return acc


def gradients(v, tab_ref):
    return (
        along_major(v, 0, False),
        along_major(v, 1, False),
        along_sublane(v, tab_ref, 0),
    )


def transposed(v, tab_ref, direction):
    if direction == 0:
        return along_major(v, 0, True)
    if direction == 1:
        return along_major(v, 1, True)
    return along_sublane(v, tab_ref, 8)


def forward_terms(q, flow, mass, kappa, tab_ref):
    g = gradients(q, tab_ref)
    advect = flow[0] * g[0] + flow[1] * g[1] + flow[2] * g[2]
    diffuse = transposed(mass * g[0], tab_ref, 0)
    diffuse = diffuse + transposed(mass * g[1], tab_ref, 1)
    diffuse = diffuse + transposed(mass * g[2], tab_ref, 2)
    return -(mass * advect) - kappa * diffuse


def adjoint_terms(q, flow, mass, kappa, tab_ref):
    g = gradients(q, tab_ref)
    summed = transposed(mass * (flow[0] * q + kappa * g[0]), tab_ref, 0)
    summed = summed + transposed(mass * (flow[1] * q + kappa * g[1]), tab_ref, 1)
    summed = summed + transposed(mass * (flow[2] * q + kappa * g[2]), tab_ref, 2)
    return -summed


def z_assemble(v):
    shape = v.shape
    sub = lax.broadcasted_iota(jnp.int32, shape, 2)
    lane = lax.broadcasted_iota(jnp.int32, shape, 3)
    below = pltpu.roll(pltpu.roll(v, 1, 2), 1, 3)
    above = pltpu.roll(pltpu.roll(v, 7, 2), 127, 3)
    zero = jnp.zeros_like(v)
    v = v + jnp.where((sub == 0) & (lane > 0), below, zero)
    return v + jnp.where((sub == 7) & (lane < 127), above, zero)


def permute(x, pm, transpose):
    bf = jnp.bfloat16
    f32 = jnp.float32
    dims = (((1,), (1,) if transpose else (0,)), ((), ()))

    def dot(a):
        return lax.dot_general(a, pm, dims, preferred_element_type=f32)

    x1 = x.astype(bf)
    r1 = x - x1.astype(f32)
    x2 = r1.astype(bf)
    x3 = (r1 - x2.astype(f32)).astype(bf)
    return dot(x1) + dot(x2) + dot(x3)


def kernel(
    ndev,
    cols,
    fld_in,
    adj_in,
    vel_in,
    mass_in,
    tab_ref,
    num_ref,
    kap_ref,
    out_f_in,
    out_a_in,
    fld_ref,
    adj_ref,
    vel_ref,
    mass_ref,
    out_f_ref,
    out_a_ref,
    ms_ref,
    f1_ref,
    a1_ref,
    xs,
    sj,
    rj,
    si,
    ri,
    sd,
    rd,
    ssem,
    rsem,
):
    me = lax.axis_index("elem")
    column = (me + cols // 2) % ndev
    place = column % cols
    row = column // cols
    right = (me + 1) % ndev
    left = (me + ndev - 1) % ndev
    up = (me + cols) % ndev
    down = (me + ndev - cols) % ndev
    has_right = place < cols - 1
    has_left = place > 0
    has_up = row < DA - 1
    has_down = row > 0

    up_right = (me + cols + 1) % ndev
    up_left = (me + cols + ndev - 1) % ndev
    down_right = (me + 2 * ndev - cols + 1) % ndev
    down_left = (me + 2 * ndev - cols - 1) % ndev

    barrier = pltpu.get_barrier_semaphore()
    for nb in (left, right, up, down, up_right, up_left, down_right, down_left):
        pl.semaphore_signal(barrier, inc=1, device_id=(nb,), device_id_type=pl.DeviceIdType.MESH)
    pl.semaphore_wait(barrier, 8)

    count = num_ref.shape[1]
    height = lax.rem(num_ref[...], count)
    p_out = (lax.broadcasted_iota(jnp.int32, (count, count), 0) == height).astype(jnp.bfloat16)

    def sort_in(src_ref, dst_ref):
        dst_ref[...] = permute(src_ref[...], p_out, True).reshape(dst_ref.shape)

    for f in range(3):
        sort_in(fld_in.at[f], fld_ref.at[f])
        sort_in(adj_in.at[f], adj_ref.at[f])
        sort_in(vel_in.at[f], vel_ref.at[f])
    sort_in(mass_in, mass_ref)
    mass_ref[...] = mass_ref[...] * tab_ref[16:80].reshape(mass_ref.shape)

    groups = ((0, 4), (4, 7), (7, 10), (10, 13))

    def plan(g):
        lo, hi = groups[g]
        n = hi - lo
        sends = [
            (sj.at[g, 1, 0:n], rj.at[g, 0, 0:n], right, has_right),
            (sj.at[g, 0, 0:n], rj.at[g, 1, 0:n], left, has_left),
            (si.at[g, 1, 0:n], ri.at[g, 0, 0:n], up, has_up),
            (si.at[g, 0, 0:n], ri.at[g, 1, 0:n], down, has_down),
            (sd.at[g, 0, 0:n], rd.at[g, 0, 0:n], up_right, has_up & has_right),
            (sd.at[g, 1, 0:n], rd.at[g, 1, 0:n], up_left, has_up & has_left),
            (sd.at[g, 2, 0:n], rd.at[g, 2, 0:n], down_right, has_down & has_right),
            (sd.at[g, 3, 0:n], rd.at[g, 3, 0:n], down_left, has_down & has_left),
        ]
        copies = [
            pltpu.make_async_remote_copy(
                s, d, ssem.at[g, k], rsem.at[g, k], device_id=(t,), device_id_type=pl.DeviceIdType.MESH
            )
            for k, (s, d, t, _) in enumerate(sends)
        ]
        recv_has = [has_left, has_right, has_down, has_up,
                    has_down & has_left, has_down & has_right, has_up & has_left, has_up & has_right]
        targets = [
            xs.at[lo:hi, :, 0], xs.at[lo:hi, :, 7], xs.at[lo:hi, 0], xs.at[lo:hi, 7],
            xs.at[lo:hi, 0, 0], xs.at[lo:hi, 0, 7], xs.at[lo:hi, 7, 0], xs.at[lo:hi, 7, 7],
        ]
        return sends, copies, recv_has, targets

    def start_group(g):
        lo, hi = groups[g]
        n = hi - lo
        for u in range(lo, hi):
            xs[u] = z_assemble(xs[u])
        sj[g, 0, 0:n] = xs[lo:hi, :, 0]
        sj[g, 1, 0:n] = xs[lo:hi, :, 7]
        si[g, 0, 0:n] = xs[lo:hi, 0]
        si[g, 1, 0:n] = xs[lo:hi, 7]
        sd[g, 0, 0:n] = xs[lo:hi, 7, 7]
        sd[g, 1, 0:n] = xs[lo:hi, 7, 0]
        sd[g, 2, 0:n] = xs[lo:hi, 0, 7]
        sd[g, 3, 0:n] = xs[lo:hi, 0, 0]
        sends, copies, _, _ = plan(g)
        for (_, _, _, has), c in zip(sends, copies):
            @pl.when(has)
            def _():
                c.start()

    def finish_group(g):
        sends, copies, recv_has, targets = plan(g)
        for (_, _, _, has), c in zip(sends, copies):
            @pl.when(has)
            def _():
                c.wait_send()
        for k in range(8):
            @pl.when(recv_has[k])
            def _():
                copies[k].wait_recv()
                targets[k][...] = targets[k][...] + sends[k][1][...]

    def flow():
        return (vel_ref[0], vel_ref[1], vel_ref[2])

    xs[0] = mass_ref[...]
    for f in range(3):
        xs[1 + f] = adj_ref[f]
    start_group(0)
    for f in range(3):
        xs[4 + f] = forward_terms(fld_ref[f], flow(), mass_ref[...], kap_ref[f], tab_ref)
    start_group(1)
    finish_group(0)
    ms_ref[...] = xs[0]
    for f in range(3):
        gathered = xs[1 + f] / ms_ref[...]
        a1 = adj_ref[f] + time_step * adjoint_terms(gathered, flow(), mass_ref[...], kap_ref[f], tab_ref)
        a1_ref[f] = a1
        xs[7 + f] = a1 / ms_ref[...]
    start_group(2)
    finish_group(1)
    for f in range(3):
        f1 = fld_ref[f] + time_step * xs[4 + f] / ms_ref[...]
        f1_ref[f] = f1
        xs[10 + f] = forward_terms(f1, flow(), mass_ref[...], kap_ref[f], tab_ref)
    start_group(3)
    finish_group(2)
    for f in range(3):
        out_a_ref[f] = a1_ref[f] + time_step * adjoint_terms(xs[7 + f], flow(), mass_ref[...], kap_ref[f], tab_ref)
    finish_group(3)
    for f in range(3):
        out_f_ref[f] = f1_ref[f] + time_step * xs[10 + f] / ms_ref[...]

    for f in range(3):
        out_f_in[f] = permute(out_f_ref[f].reshape(512, 128), p_out, False)
        out_a_in[f] = permute(out_a_ref[f].reshape(512, 128), p_out, False)


def fused(fields, adjoint, flow, mass, table, numbering, kappa, ndev, cols):
    cube = (8, 8, 8, 128)
    f32 = jnp.float32
    units = 13
    vmem = pl.BlockSpec(memory_space=pltpu.VMEM)
    smem = pl.BlockSpec(memory_space=pltpu.SMEM)
    scratch = [
        pltpu.VMEM((3,) + cube, f32),
        pltpu.VMEM((3,) + cube, f32),
        pltpu.VMEM((3,) + cube, f32),
        pltpu.VMEM(cube, f32),
        pltpu.VMEM((3,) + cube, f32),
        pltpu.VMEM((3,) + cube, f32),
        pltpu.VMEM(cube, f32),
        pltpu.VMEM((3,) + cube, f32),
        pltpu.VMEM((3,) + cube, f32),
        pltpu.VMEM((units,) + cube, f32),
    ]
    groups = 4
    for _ in range(4):
        scratch.append(pltpu.VMEM((groups, 2, 4, 8, 8, 128), f32))
    for _ in range(2):
        scratch.append(pltpu.VMEM((groups, 4, 4, 8, 128), f32))
    scratch += [pltpu.SemaphoreType.DMA((groups, 8)), pltpu.SemaphoreType.DMA((groups, 8))]
    shape = fields.shape
    return pl.pallas_call(
        functools.partial(kernel, ndev, cols),
        out_shape=(jax.ShapeDtypeStruct(shape, f32), jax.ShapeDtypeStruct(shape, f32)),
        in_specs=[vmem, vmem, vmem, vmem, vmem, vmem, smem],
        out_specs=(vmem, vmem),
        scratch_shapes=scratch,
        compiler_params=pltpu.CompilerParams(
            collective_id=0, has_side_effects=True, vmem_limit_bytes=60 * 1024 * 1024
        ),
    )(fields, adjoint, flow, mass, table, numbering, kappa)


def shards(moment_fields, adjoint_fields, velocity, mass_weights, diffusivity, numbering):
    ndev = lax.axis_size("elem")
    cols = ndev // DA
    table = jnp.asarray(shift_tables())
    return fused(
        moment_fields, adjoint_fields, velocity, mass_weights, table,
        numbering.reshape(1, -1), diffusivity, ndev, cols,
    )


def solution(mesh):
    in_specs = (
        P(None, None, "elem"),
        P(None, None, "elem"),
        P(None, None, "elem"),
        P(None, "elem"),
        P(),
        P("elem"),
    )
    out_specs = (P(None, None, "elem"), P(None, None, "elem"))
    return jax.shard_map(shards, mesh=mesh, in_specs=in_specs, out_specs=out_specs, check_vma=False)
```

```python
import functools

import jax
import jax.numpy as jnp
import numpy as np
from jax import lax
from jax.experimental import pallas as pl
from jax.experimental.pallas import tpu as pltpu
from jax.sharding import PartitionSpec as P

DA = 4

time_step = 0.001


def gll_tables():
    points = [
        -1.0,
        -0.8717401485096066,
        -0.5917001814331423,
        -0.2092992179024789,
        0.2092992179024789,
        0.5917001814331423,
        0.8717401485096066,
        1.0,
    ]
    weights = [
        0.03571428571428571,
        0.21070422714350603,
        0.3411226924835044,
        0.4124587946587038,
        0.4124587946587038,
        0.3411226924835044,
        0.21070422714350603,
        0.03571428571428571,
    ]
    barycentric = []
    for left_index in range(8):
        product = 1.0
        for right_index in range(8):
            if right_index != left_index:
                product = product * (points[left_index] - points[right_index])
        barycentric.append(1.0 / product)
    derivative = np.zeros((8, 8))
    for left_index in range(8):
        row_total = 0.0
        for right_index in range(8):
            if left_index != right_index:
                entry = (
                    barycentric[right_index]
                    / barycentric[left_index]
                    / (points[left_index] - points[right_index])
                )
                derivative[left_index, right_index] = entry
                row_total = row_total + entry
        derivative[left_index, left_index] = -row_total
    return derivative.astype(np.float32), np.asarray(weights, dtype=np.float32)


DM, WEIGHTS = gll_tables()
DMC = [[float(DM[p, q]) for q in range(8)] for p in range(8)]


def shift_tables():
    fwd = np.zeros((8, 8, 128), np.float32)
    bwd = np.zeros((8, 8, 128), np.float32)
    for s in range(8):
        for p in range(8):
            fwd[s, p, :] = DM[p, (p - s) % 8]
            bwd[s, p, :] = DM[(p - s) % 8, p]
    cube = (WEIGHTS[:, None, None] * WEIGHTS[None, :, None]) * WEIGHTS[None, None, :]
    wrows = np.broadcast_to(cube.reshape(64, 8, 1), (64, 8, 128)).astype(np.float32)
    return np.concatenate([fwd, bwd, wrows], axis=0)


def along_major(v, axis, transpose):
    parts = []
    for p in range(8):
        acc = None
        for q in range(8):
            c = DMC[q][p] if transpose else DMC[p][q]
            term = c * (v[q] if axis == 0 else v[:, q])
            acc = term if acc is None else acc + term
        parts.append(acc)
    return jnp.stack(parts, axis=axis)


def along_sublane(v, tab_ref, base):
    acc = None
    for s in range(8):
        rolled = v if s == 0 else pltpu.roll(v, s, 2)
        term = tab_ref[base + s] * rolled
        acc = term if acc is None else acc + term
    return acc


def gradients(v, tab_ref):
    return (
        along_major(v, 0, False),
        along_major(v, 1, False),
        along_sublane(v, tab_ref, 0),
    )


def transposed(v, tab_ref, direction):
    if direction == 0:
        return along_major(v, 0, True)
    if direction == 1:
        return along_major(v, 1, True)
    return along_sublane(v, tab_ref, 8)


def forward_terms(q, flow, mass, kappa, tab_ref):
    g = gradients(q, tab_ref)
    advect = flow[0] * g[0] + flow[1] * g[1] + flow[2] * g[2]
    diffuse = transposed(mass * g[0], tab_ref, 0)
    diffuse = diffuse + transposed(mass * g[1], tab_ref, 1)
    diffuse = diffuse + transposed(mass * g[2], tab_ref, 2)
    return -(mass * advect) - kappa * diffuse


def adjoint_terms(q, flow, mass, kappa, tab_ref):
    g = gradients(q, tab_ref)
    summed = transposed(mass * (flow[0] * q + kappa * g[0]), tab_ref, 0)
    summed = summed + transposed(mass * (flow[1] * q + kappa * g[1]), tab_ref, 1)
    summed = summed + transposed(mass * (flow[2] * q + kappa * g[2]), tab_ref, 2)
    return -summed


def z_assemble(v):
    shape = v.shape
    sub = lax.broadcasted_iota(jnp.int32, shape, 2)
    lane = lax.broadcasted_iota(jnp.int32, shape, 3)
    below = pltpu.roll(pltpu.roll(v, 1, 2), 1, 3)
    above = pltpu.roll(pltpu.roll(v, 7, 2), 127, 3)
    zero = jnp.zeros_like(v)
    v = v + jnp.where((sub == 0) & (lane > 0), below, zero)
    return v + jnp.where((sub == 7) & (lane < 127), above, zero)


def permute(x, pm, transpose):
    bf = jnp.bfloat16
    f32 = jnp.float32
    dims = (((1,), (1,) if transpose else (0,)), ((), ()))

    def dot(a):
        return lax.dot_general(a, pm, dims, preferred_element_type=f32)

    x1 = x.astype(bf)
    r1 = x - x1.astype(f32)
    x2 = r1.astype(bf)
    x3 = (r1 - x2.astype(f32)).astype(bf)
    return dot(x1) + dot(x2) + dot(x3)


def kernel(
    ndev,
    cols,
    fld_in,
    adj_in,
    vel_in,
    mass_in,
    tab_ref,
    num_ref,
    kap_ref,
    out_f_in,
    out_a_in,
    fld_ref,
    adj_ref,
    vel_ref,
    mass_ref,
    out_f_ref,
    out_a_ref,
    ms_ref,
    f1_ref,
    a1_ref,
    xs,
    sj,
    rj,
    si,
    ri,
    sd,
    rd,
    ssem,
    rsem,
):
    me = lax.axis_index("elem")
    column = (me + cols // 2) % ndev
    place = column % cols
    row = column // cols
    right = (me + 1) % ndev
    left = (me + ndev - 1) % ndev
    up = (me + cols) % ndev
    down = (me + ndev - cols) % ndev
    has_right = place < cols - 1
    has_left = place > 0
    has_up = row < DA - 1
    has_down = row > 0

    up_right = (me + cols + 1) % ndev
    up_left = (me + cols + ndev - 1) % ndev
    down_right = (me + 2 * ndev - cols + 1) % ndev
    down_left = (me + 2 * ndev - cols - 1) % ndev

    barrier = pltpu.get_barrier_semaphore()
    for nb in (left, right, up, down, up_right, up_left, down_right, down_left):
        pl.semaphore_signal(barrier, inc=1, device_id=(nb,), device_id_type=pl.DeviceIdType.MESH)

    count = num_ref.shape[1]
    height = lax.rem(num_ref[...], count)
    p_out = (lax.broadcasted_iota(jnp.int32, (count, count), 0) == height).astype(jnp.bfloat16)

    def sort_in(src_ref, dst_ref):
        dst_ref[...] = permute(src_ref[...], p_out, True).reshape(dst_ref.shape)

    for f in range(3):
        sort_in(adj_in.at[f], adj_ref.at[f])
    sort_in(mass_in, mass_ref)
    mass_ref[...] = mass_ref[...] * tab_ref[16:80].reshape(mass_ref.shape)

    groups = ((0, 4), (4, 7), (7, 10), (10, 13))

    def plan(g):
        lo, hi = groups[g]
        n = hi - lo
        sends = [
            (sj.at[g, 1, 0:n], rj.at[g, 0, 0:n], right, has_right),
            (sj.at[g, 0, 0:n], rj.at[g, 1, 0:n], left, has_left),
            (si.at[g, 1, 0:n], ri.at[g, 0, 0:n], up, has_up),
            (si.at[g, 0, 0:n], ri.at[g, 1, 0:n], down, has_down),
            (sd.at[g, 0, 0:n], rd.at[g, 0, 0:n], up_right, has_up & has_right),
            (sd.at[g, 1, 0:n], rd.at[g, 1, 0:n], up_left, has_up & has_left),
            (sd.at[g, 2, 0:n], rd.at[g, 2, 0:n], down_right, has_down & has_right),
            (sd.at[g, 3, 0:n], rd.at[g, 3, 0:n], down_left, has_down & has_left),
        ]
        copies = [
            pltpu.make_async_remote_copy(
                s, d, ssem.at[g, k], rsem.at[g, k], device_id=(t,), device_id_type=pl.DeviceIdType.MESH
            )
            for k, (s, d, t, _) in enumerate(sends)
        ]
        recv_has = [has_left, has_right, has_down, has_up,
                    has_down & has_left, has_down & has_right, has_up & has_left, has_up & has_right]
        targets = [
            xs.at[lo:hi, :, 0], xs.at[lo:hi, :, 7], xs.at[lo:hi, 0], xs.at[lo:hi, 7],
            xs.at[lo:hi, 0, 0], xs.at[lo:hi, 0, 7], xs.at[lo:hi, 7, 0], xs.at[lo:hi, 7, 7],
        ]
        return sends, copies, recv_has, targets

    def start_group(g):
        prep_group(g)
        launch_group(g)

    def prep_group(g):
        lo, hi = groups[g]
        n = hi - lo
        for u in range(lo, hi):
            xs[u] = z_assemble(xs[u])
        sj[g, 0, 0:n] = xs[lo:hi, :, 0]
        sj[g, 1, 0:n] = xs[lo:hi, :, 7]
        si[g, 0, 0:n] = xs[lo:hi, 0]
        si[g, 1, 0:n] = xs[lo:hi, 7]
        sd[g, 0, 0:n] = xs[lo:hi, 7, 7]
        sd[g, 1, 0:n] = xs[lo:hi, 7, 0]
        sd[g, 2, 0:n] = xs[lo:hi, 0, 7]
        sd[g, 3, 0:n] = xs[lo:hi, 0, 0]

    def launch_group(g):
        sends, copies, _, _ = plan(g)
        for (_, _, _, has), c in zip(sends, copies):
            @pl.when(has)
            def _():
                c.start()

    def finish_group(g):
        sends, copies, recv_has, targets = plan(g)
        for (_, _, _, has), c in zip(sends, copies):
            @pl.when(has)
            def _():
                c.wait_send()
        for k in range(8):
            @pl.when(recv_has[k])
            def _():
                copies[k].wait_recv()
                targets[k][...] = targets[k][...] + sends[k][1][...]

    def flow():
        return (vel_ref[0], vel_ref[1], vel_ref[2])

    xs[0] = mass_ref[...]
    for f in range(3):
        xs[1 + f] = adj_ref[f]
    prep_group(0)
    pl.semaphore_wait(barrier, 8)
    launch_group(0)
    for f in range(3):
        sort_in(fld_in.at[f], fld_ref.at[f])
        sort_in(vel_in.at[f], vel_ref.at[f])
    for f in range(3):
        xs[4 + f] = forward_terms(fld_ref[f], flow(), mass_ref[...], kap_ref[f], tab_ref)
    start_group(1)
    finish_group(0)
    ms_ref[...] = xs[0]
    for f in range(3):
        gathered = xs[1 + f] / ms_ref[...]
        a1 = adj_ref[f] + time_step * adjoint_terms(gathered, flow(), mass_ref[...], kap_ref[f], tab_ref)
        a1_ref[f] = a1
        xs[7 + f] = a1 / ms_ref[...]
    start_group(2)
    finish_group(1)
    for f in range(3):
        f1 = fld_ref[f] + time_step * xs[4 + f] / ms_ref[...]
        f1_ref[f] = f1
        xs[10 + f] = forward_terms(f1, flow(), mass_ref[...], kap_ref[f], tab_ref)
    start_group(3)
    finish_group(2)
    for f in range(3):
        out_a_ref[f] = a1_ref[f] + time_step * adjoint_terms(xs[7 + f], flow(), mass_ref[...], kap_ref[f], tab_ref)
    for f in range(3):
        out_a_in[f] = permute(out_a_ref[f].reshape(512, 128), p_out, False)
    finish_group(3)
    for f in range(3):
        out_f_ref[f] = f1_ref[f] + time_step * xs[10 + f] / ms_ref[...]
        out_f_in[f] = permute(out_f_ref[f].reshape(512, 128), p_out, False)


def fused(fields, adjoint, flow, mass, table, numbering, kappa, ndev, cols):
    cube = (8, 8, 8, 128)
    f32 = jnp.float32
    units = 13
    vmem = pl.BlockSpec(memory_space=pltpu.VMEM)
    smem = pl.BlockSpec(memory_space=pltpu.SMEM)
    scratch = [
        pltpu.VMEM((3,) + cube, f32),
        pltpu.VMEM((3,) + cube, f32),
        pltpu.VMEM((3,) + cube, f32),
        pltpu.VMEM(cube, f32),
        pltpu.VMEM((3,) + cube, f32),
        pltpu.VMEM((3,) + cube, f32),
        pltpu.VMEM(cube, f32),
        pltpu.VMEM((3,) + cube, f32),
        pltpu.VMEM((3,) + cube, f32),
        pltpu.VMEM((units,) + cube, f32),
    ]
    groups = 4
    for _ in range(4):
        scratch.append(pltpu.VMEM((groups, 2, 4, 8, 8, 128), f32))
    for _ in range(2):
        scratch.append(pltpu.VMEM((groups, 4, 4, 8, 128), f32))
    scratch += [pltpu.SemaphoreType.DMA((groups, 8)), pltpu.SemaphoreType.DMA((groups, 8))]
    shape = fields.shape
    return pl.pallas_call(
        functools.partial(kernel, ndev, cols),
        out_shape=(jax.ShapeDtypeStruct(shape, f32), jax.ShapeDtypeStruct(shape, f32)),
        in_specs=[vmem, vmem, vmem, vmem, vmem, vmem, smem],
        out_specs=(vmem, vmem),
        scratch_shapes=scratch,
        compiler_params=pltpu.CompilerParams(
            collective_id=0, has_side_effects=True, vmem_limit_bytes=60 * 1024 * 1024
        ),
    )(fields, adjoint, flow, mass, table, numbering, kappa)


def shards(moment_fields, adjoint_fields, velocity, mass_weights, diffusivity, numbering):
    ndev = lax.axis_size("elem")
    cols = ndev // DA
    table = jnp.asarray(shift_tables())
    return fused(
        moment_fields, adjoint_fields, velocity, mass_weights, table,
        numbering.reshape(1, -1), diffusivity, ndev, cols,
    )


def solution(mesh):
    in_specs = (
        P(None, None, "elem"),
        P(None, None, "elem"),
        P(None, None, "elem"),
        P(None, "elem"),
        P(),
        P("elem"),
    )
    out_specs = (P(None, None, "elem"), P(None, None, "elem"))
    return jax.shard_map(shards, mesh=mesh, in_specs=in_specs, out_specs=out_specs, check_vma=False)
```

```python
import functools

import jax
import jax.numpy as jnp
import numpy as np
from jax import lax
from jax.experimental import pallas as pl
from jax.experimental.pallas import tpu as pltpu
from jax.sharding import PartitionSpec as P

DA = 4

time_step = 0.001


def gll_tables():
    points = [
        -1.0,
        -0.8717401485096066,
        -0.5917001814331423,
        -0.2092992179024789,
        0.2092992179024789,
        0.5917001814331423,
        0.8717401485096066,
        1.0,
    ]
    weights = [
        0.03571428571428571,
        0.21070422714350603,
        0.3411226924835044,
        0.4124587946587038,
        0.4124587946587038,
        0.3411226924835044,
        0.21070422714350603,
        0.03571428571428571,
    ]
    barycentric = []
    for left_index in range(8):
        product = 1.0
        for right_index in range(8):
            if right_index != left_index:
                product = product * (points[left_index] - points[right_index])
        barycentric.append(1.0 / product)
    derivative = np.zeros((8, 8))
    for left_index in range(8):
        row_total = 0.0
        for right_index in range(8):
            if left_index != right_index:
                entry = (
                    barycentric[right_index]
                    / barycentric[left_index]
                    / (points[left_index] - points[right_index])
                )
                derivative[left_index, right_index] = entry
                row_total = row_total + entry
        derivative[left_index, left_index] = -row_total
    return derivative.astype(np.float32), np.asarray(weights, dtype=np.float32)


DM, WEIGHTS = gll_tables()
DMC = [[float(DM[p, q]) for q in range(8)] for p in range(8)]


def shift_tables():
    fwd = np.zeros((8, 8, 128), np.float32)
    bwd = np.zeros((8, 8, 128), np.float32)
    for s in range(8):
        for p in range(8):
            fwd[s, p, :] = DM[p, (p - s) % 8]
            bwd[s, p, :] = DM[(p - s) % 8, p]
    cube = (WEIGHTS[:, None, None] * WEIGHTS[None, :, None]) * WEIGHTS[None, None, :]
    wrows = np.broadcast_to(cube.reshape(64, 8, 1), (64, 8, 128)).astype(np.float32)
    return np.concatenate([fwd, bwd, wrows], axis=0)


def along_major(v, axis, transpose):
    parts = []
    for p in range(8):
        acc = None
        for q in range(8):
            c = DMC[q][p] if transpose else DMC[p][q]
            term = c * (v[q] if axis == 0 else v[:, q])
            acc = term if acc is None else acc + term
        parts.append(acc)
    return jnp.stack(parts, axis=axis)


def along_sublane(v, tab_ref, base):
    acc = None
    for s in range(8):
        rolled = v if s == 0 else pltpu.roll(v, s, 2)
        term = tab_ref[base + s] * rolled
        acc = term if acc is None else acc + term
    return acc


def gradients(v, tab_ref):
    return (
        along_major(v, 0, False),
        along_major(v, 1, False),
        along_sublane(v, tab_ref, 0),
    )


def transposed(v, tab_ref, direction):
    if direction == 0:
        return along_major(v, 0, True)
    if direction == 1:
        return along_major(v, 1, True)
    return along_sublane(v, tab_ref, 8)


def forward_terms(q, flow, mass, kappa, tab_ref):
    g = gradients(q, tab_ref)
    advect = flow[0] * g[0] + flow[1] * g[1] + flow[2] * g[2]
    diffuse = transposed(mass * g[0], tab_ref, 0)
    diffuse = diffuse + transposed(mass * g[1], tab_ref, 1)
    diffuse = diffuse + transposed(mass * g[2], tab_ref, 2)
    return -(mass * advect) - kappa * diffuse


def adjoint_terms(q, flow, mass, kappa, tab_ref):
    g = gradients(q, tab_ref)
    summed = transposed(mass * (flow[0] * q + kappa * g[0]), tab_ref, 0)
    summed = summed + transposed(mass * (flow[1] * q + kappa * g[1]), tab_ref, 1)
    summed = summed + transposed(mass * (flow[2] * q + kappa * g[2]), tab_ref, 2)
    return -summed


def z_assemble(v):
    shape = v.shape
    sub = lax.broadcasted_iota(jnp.int32, shape, 2)
    lane = lax.broadcasted_iota(jnp.int32, shape, 3)
    below = pltpu.roll(pltpu.roll(v, 1, 2), 1, 3)
    above = pltpu.roll(pltpu.roll(v, 7, 2), 127, 3)
    zero = jnp.zeros_like(v)
    v = v + jnp.where((sub == 0) & (lane > 0), below, zero)
    return v + jnp.where((sub == 7) & (lane < 127), above, zero)


def permute(x, pm, transpose):
    bf = jnp.bfloat16
    f32 = jnp.float32
    dims = (((1,), (1,) if transpose else (0,)), ((), ()))

    def dot(a):
        return lax.dot_general(a, pm, dims, preferred_element_type=f32)

    x1 = x.astype(bf)
    r1 = x - x1.astype(f32)
    x2 = r1.astype(bf)
    x3 = (r1 - x2.astype(f32)).astype(bf)
    return dot(x1) + dot(x2) + dot(x3)


def kernel(
    ndev,
    cols,
    fld_in,
    adj_in,
    vel_in,
    mass_in,
    tab_ref,
    num_ref,
    kap_ref,
    out_f_in,
    out_a_in,
    fld_ref,
    adj_ref,
    vel_ref,
    mass_ref,
    out_f_ref,
    out_a_ref,
    ms_ref,
    f1_ref,
    a1_ref,
    xs,
    sj,
    rj,
    si,
    ri,
    sd,
    rd,
    ssem,
    rsem,
):
    me = lax.axis_index("elem")
    column = (me + cols // 2) % ndev
    place = column % cols
    row = column // cols
    right = (me + 1) % ndev
    left = (me + ndev - 1) % ndev
    up = (me + cols) % ndev
    down = (me + ndev - cols) % ndev
    has_right = place < cols - 1
    has_left = place > 0
    has_up = row < DA - 1
    has_down = row > 0

    up_right = (me + cols + 1) % ndev
    up_left = (me + cols + ndev - 1) % ndev
    down_right = (me + 2 * ndev - cols + 1) % ndev
    down_left = (me + 2 * ndev - cols - 1) % ndev

    barrier = pltpu.get_barrier_semaphore()
    for nb in (left, right, up, down, up_right, up_left, down_right, down_left):
        pl.semaphore_signal(barrier, inc=1, device_id=(nb,), device_id_type=pl.DeviceIdType.MESH)

    count = num_ref.shape[1]
    height = lax.rem(num_ref[...], count)
    p_out = (lax.broadcasted_iota(jnp.int32, (count, count), 0) == height).astype(jnp.bfloat16)

    def sort_in(src_ref, dst_ref):
        dst_ref[...] = permute(src_ref[...], p_out, True).reshape(dst_ref.shape)

    for f in range(3):
        sort_in(adj_in.at[f], adj_ref.at[f])
    sort_in(mass_in, mass_ref)
    mass_ref[...] = mass_ref[...] * tab_ref[16:80].reshape(mass_ref.shape)

    groups = ((0, 4),) + tuple((u, u + 1) for u in range(4, 13))

    def plan(g):
        lo, hi = groups[g]
        n = hi - lo
        sends = [
            (sj.at[g, 1, 0:n], rj.at[g, 0, 0:n], right, has_right),
            (sj.at[g, 0, 0:n], rj.at[g, 1, 0:n], left, has_left),
            (si.at[g, 1, 0:n], ri.at[g, 0, 0:n], up, has_up),
            (si.at[g, 0, 0:n], ri.at[g, 1, 0:n], down, has_down),
            (sd.at[g, 0, 0:n], rd.at[g, 0, 0:n], up_right, has_up & has_right),
            (sd.at[g, 1, 0:n], rd.at[g, 1, 0:n], up_left, has_up & has_left),
            (sd.at[g, 2, 0:n], rd.at[g, 2, 0:n], down_right, has_down & has_right),
            (sd.at[g, 3, 0:n], rd.at[g, 3, 0:n], down_left, has_down & has_left),
        ]
        copies = [
            pltpu.make_async_remote_copy(
                s, d, ssem.at[g, k], rsem.at[g, k], device_id=(t,), device_id_type=pl.DeviceIdType.MESH
            )
            for k, (s, d, t, _) in enumerate(sends)
        ]
        recv_has = [has_left, has_right, has_down, has_up,
                    has_down & has_left, has_down & has_right, has_up & has_left, has_up & has_right]
        targets = [
            xs.at[lo:hi, :, 0], xs.at[lo:hi, :, 7], xs.at[lo:hi, 0], xs.at[lo:hi, 7],
            xs.at[lo:hi, 0, 0], xs.at[lo:hi, 0, 7], xs.at[lo:hi, 7, 0], xs.at[lo:hi, 7, 7],
        ]
        return sends, copies, recv_has, targets

    def start_group(g):
        prep_group(g)
        launch_group(g)

    def prep_group(g):
        lo, hi = groups[g]
        n = hi - lo
        for u in range(lo, hi):
            xs[u] = z_assemble(xs[u])
        sj[g, 0, 0:n] = xs[lo:hi, :, 0]
        sj[g, 1, 0:n] = xs[lo:hi, :, 7]
        si[g, 0, 0:n] = xs[lo:hi, 0]
        si[g, 1, 0:n] = xs[lo:hi, 7]
        sd[g, 0, 0:n] = xs[lo:hi, 7, 7]
        sd[g, 1, 0:n] = xs[lo:hi, 7, 0]
        sd[g, 2, 0:n] = xs[lo:hi, 0, 7]
        sd[g, 3, 0:n] = xs[lo:hi, 0, 0]

    def launch_group(g):
        sends, copies, _, _ = plan(g)
        for (_, _, _, has), c in zip(sends, copies):
            @pl.when(has)
            def _():
                c.start()

    def finish_group(g):
        sends, copies, recv_has, targets = plan(g)
        for (_, _, _, has), c in zip(sends, copies):
            @pl.when(has)
            def _():
                c.wait_send()
        for k in range(8):
            @pl.when(recv_has[k])
            def _():
                copies[k].wait_recv()
                targets[k][...] = targets[k][...] + sends[k][1][...]

    def flow():
        return (vel_ref[0], vel_ref[1], vel_ref[2])

    xs[0] = mass_ref[...]
    for f in range(3):
        xs[1 + f] = adj_ref[f]
    prep_group(0)
    pl.semaphore_wait(barrier, 8)
    launch_group(0)
    for f in range(3):
        sort_in(fld_in.at[f], fld_ref.at[f])
        sort_in(vel_in.at[f], vel_ref.at[f])
    for f in range(3):
        xs[4 + f] = forward_terms(fld_ref[f], flow(), mass_ref[...], kap_ref[f], tab_ref)
        start_group(1 + f)
    finish_group(0)
    ms_ref[...] = xs[0]
    for f in range(3):
        gathered = xs[1 + f] / ms_ref[...]
        a1 = adj_ref[f] + time_step * adjoint_terms(gathered, flow(), mass_ref[...], kap_ref[f], tab_ref)
        a1_ref[f] = a1
        xs[7 + f] = a1 / ms_ref[...]
        start_group(4 + f)
    for f in range(3):
        finish_group(1 + f)
        f1 = fld_ref[f] + time_step * xs[4 + f] / ms_ref[...]
        f1_ref[f] = f1
        xs[10 + f] = forward_terms(f1, flow(), mass_ref[...], kap_ref[f], tab_ref)
        start_group(7 + f)
    for f in range(3):
        finish_group(4 + f)
        out_a_ref[f] = a1_ref[f] + time_step * adjoint_terms(xs[7 + f], flow(), mass_ref[...], kap_ref[f], tab_ref)
        out_a_in[f] = permute(out_a_ref[f].reshape(512, 128), p_out, False)
    for f in range(3):
        finish_group(7 + f)
        out_f_ref[f] = f1_ref[f] + time_step * xs[10 + f] / ms_ref[...]
        out_f_in[f] = permute(out_f_ref[f].reshape(512, 128), p_out, False)


def fused(fields, adjoint, flow, mass, table, numbering, kappa, ndev, cols):
    cube = (8, 8, 8, 128)
    f32 = jnp.float32
    units = 13
    vmem = pl.BlockSpec(memory_space=pltpu.VMEM)
    smem = pl.BlockSpec(memory_space=pltpu.SMEM)
    scratch = [
        pltpu.VMEM((3,) + cube, f32),
        pltpu.VMEM((3,) + cube, f32),
        pltpu.VMEM((3,) + cube, f32),
        pltpu.VMEM(cube, f32),
        pltpu.VMEM((3,) + cube, f32),
        pltpu.VMEM((3,) + cube, f32),
        pltpu.VMEM(cube, f32),
        pltpu.VMEM((3,) + cube, f32),
        pltpu.VMEM((3,) + cube, f32),
        pltpu.VMEM((units,) + cube, f32),
    ]
    groups = 10
    for _ in range(4):
        scratch.append(pltpu.VMEM((groups, 2, 4, 8, 8, 128), f32))
    for _ in range(2):
        scratch.append(pltpu.VMEM((groups, 4, 4, 8, 128), f32))
    scratch += [pltpu.SemaphoreType.DMA((groups, 8)), pltpu.SemaphoreType.DMA((groups, 8))]
    shape = fields.shape
    return pl.pallas_call(
        functools.partial(kernel, ndev, cols),
        out_shape=(jax.ShapeDtypeStruct(shape, f32), jax.ShapeDtypeStruct(shape, f32)),
        in_specs=[vmem, vmem, vmem, vmem, vmem, vmem, smem],
        out_specs=(vmem, vmem),
        scratch_shapes=scratch,
        compiler_params=pltpu.CompilerParams(
            collective_id=0, has_side_effects=True, vmem_limit_bytes=60 * 1024 * 1024
        ),
    )(fields, adjoint, flow, mass, table, numbering, kappa)


def shards(moment_fields, adjoint_fields, velocity, mass_weights, diffusivity, numbering):
    ndev = lax.axis_size("elem")
    cols = ndev // DA
    table = jnp.asarray(shift_tables())
    return fused(
        moment_fields, adjoint_fields, velocity, mass_weights, table,
        numbering.reshape(1, -1), diffusivity, ndev, cols,
    )


def solution(mesh):
    in_specs = (
        P(None, None, "elem"),
        P(None, None, "elem"),
        P(None, None, "elem"),
        P(None, "elem"),
        P(),
        P("elem"),
    )
    out_specs = (P(None, None, "elem"), P(None, None, "elem"))
    return jax.shard_map(shards, mesh=mesh, in_specs=in_specs, out_specs=out_specs, check_vma=False)
```

```python
import functools

import jax
import jax.numpy as jnp
import numpy as np
from jax import lax
from jax.experimental import pallas as pl
from jax.experimental.pallas import tpu as pltpu
from jax.sharding import PartitionSpec as P

DA = 4

time_step = 0.001


def gll_tables():
    points = [
        -1.0,
        -0.8717401485096066,
        -0.5917001814331423,
        -0.2092992179024789,
        0.2092992179024789,
        0.5917001814331423,
        0.8717401485096066,
        1.0,
    ]
    weights = [
        0.03571428571428571,
        0.21070422714350603,
        0.3411226924835044,
        0.4124587946587038,
        0.4124587946587038,
        0.3411226924835044,
        0.21070422714350603,
        0.03571428571428571,
    ]
    barycentric = []
    for left_index in range(8):
        product = 1.0
        for right_index in range(8):
            if right_index != left_index:
                product = product * (points[left_index] - points[right_index])
        barycentric.append(1.0 / product)
    derivative = np.zeros((8, 8))
    for left_index in range(8):
        row_total = 0.0
        for right_index in range(8):
            if left_index != right_index:
                entry = (
                    barycentric[right_index]
                    / barycentric[left_index]
                    / (points[left_index] - points[right_index])
                )
                derivative[left_index, right_index] = entry
                row_total = row_total + entry
        derivative[left_index, left_index] = -row_total
    return derivative.astype(np.float32), np.asarray(weights, dtype=np.float32)


DM, WEIGHTS = gll_tables()
DMC = [[float(DM[p, q]) for q in range(8)] for p in range(8)]


def shift_tables():
    fwd = np.zeros((8, 8, 128), np.float32)
    bwd = np.zeros((8, 8, 128), np.float32)
    for s in range(8):
        for p in range(8):
            fwd[s, p, :] = DM[p, (p - s) % 8]
            bwd[s, p, :] = DM[(p - s) % 8, p]
    cube = (WEIGHTS[:, None, None] * WEIGHTS[None, :, None]) * WEIGHTS[None, None, :]
    wrows = np.broadcast_to(cube.reshape(64, 8, 1), (64, 8, 128)).astype(np.float32)
    return np.concatenate([fwd, bwd, wrows], axis=0)


def along_major(v, axis, transpose):
    parts = []
    for p in range(8):
        acc = None
        for q in range(8):
            c = DMC[q][p] if transpose else DMC[p][q]
            term = c * (v[q] if axis == 0 else v[:, q])
            acc = term if acc is None else acc + term
        parts.append(acc)
    return jnp.stack(parts, axis=axis)


def along_sublane(v, tab_ref, base):
    acc = None
    for s in range(8):
        rolled = v if s == 0 else pltpu.roll(v, s, 2)
        term = tab_ref[base + s] * rolled
        acc = term if acc is None else acc + term
    return acc


def gradients(v, tab_ref):
    return (
        along_major(v, 0, False),
        along_major(v, 1, False),
        along_sublane(v, tab_ref, 0),
    )


def transposed(v, tab_ref, direction):
    if direction == 0:
        return along_major(v, 0, True)
    if direction == 1:
        return along_major(v, 1, True)
    return along_sublane(v, tab_ref, 8)


def forward_terms(q, flow, mass, kappa, tab_ref):
    g = gradients(q, tab_ref)
    advect = flow[0] * g[0] + flow[1] * g[1] + flow[2] * g[2]
    diffuse = transposed(mass * g[0], tab_ref, 0)
    diffuse = diffuse + transposed(mass * g[1], tab_ref, 1)
    diffuse = diffuse + transposed(mass * g[2], tab_ref, 2)
    return -(mass * advect) - kappa * diffuse


def adjoint_terms(q, flow, mass, kappa, tab_ref):
    g = gradients(q, tab_ref)
    summed = transposed(mass * (flow[0] * q + kappa * g[0]), tab_ref, 0)
    summed = summed + transposed(mass * (flow[1] * q + kappa * g[1]), tab_ref, 1)
    summed = summed + transposed(mass * (flow[2] * q + kappa * g[2]), tab_ref, 2)
    return -summed


def z_assemble(v):
    shape = v.shape
    sub = lax.broadcasted_iota(jnp.int32, shape, 2)
    lane = lax.broadcasted_iota(jnp.int32, shape, 3)
    below = pltpu.roll(pltpu.roll(v, 1, 2), 1, 3)
    above = pltpu.roll(pltpu.roll(v, 7, 2), 127, 3)
    zero = jnp.zeros_like(v)
    v = v + jnp.where((sub == 0) & (lane > 0), below, zero)
    return v + jnp.where((sub == 7) & (lane < 127), above, zero)


def permute(x, pm, transpose):
    bf = jnp.bfloat16
    f32 = jnp.float32
    dims = (((1,), (1,) if transpose else (0,)), ((), ()))

    def dot(a):
        return lax.dot_general(a, pm, dims, preferred_element_type=f32)

    x1 = x.astype(bf)
    r1 = x - x1.astype(f32)
    x2 = r1.astype(bf)
    x3 = (r1 - x2.astype(f32)).astype(bf)
    return dot(x1) + dot(x2) + dot(x3)


def kernel(
    ndev,
    cols,
    fld_in,
    adj_in,
    vel_in,
    mass_in,
    tab_ref,
    num_ref,
    kap_ref,
    out_f_in,
    out_a_in,
    fld_ref,
    adj_ref,
    vel_ref,
    mass_ref,
    out_f_ref,
    out_a_ref,
    ms_ref,
    f1_ref,
    a1_ref,
    xs,
    sj,
    rj,
    si,
    ri,
    sd,
    rd,
    ssem,
    rsem,
):
    me = lax.axis_index("elem")
    column = (me + cols // 2) % ndev
    place = column % cols
    row = column // cols
    right = (me + 1) % ndev
    left = (me + ndev - 1) % ndev
    up = (me + cols) % ndev
    down = (me + ndev - cols) % ndev
    has_right = place < cols - 1
    has_left = place > 0
    has_up = row < DA - 1
    has_down = row > 0

    up_right = (me + cols + 1) % ndev
    up_left = (me + cols + ndev - 1) % ndev
    down_right = (me + 2 * ndev - cols + 1) % ndev
    down_left = (me + 2 * ndev - cols - 1) % ndev

    barrier = pltpu.get_barrier_semaphore()
    for nb in (left, right, up, down, up_right, up_left, down_right, down_left):
        pl.semaphore_signal(barrier, inc=1, device_id=(nb,), device_id_type=pl.DeviceIdType.MESH)

    count = num_ref.shape[1]
    height = lax.rem(num_ref[...], count)
    p_out = (lax.broadcasted_iota(jnp.int32, (count, count), 0) == height).astype(jnp.bfloat16)

    def sort_in(src_ref, dst_ref):
        dst_ref[...] = permute(src_ref[...], p_out, True).reshape(dst_ref.shape)

    for f in range(3):
        sort_in(adj_in.at[f], adj_ref.at[f])
    sort_in(mass_in, mass_ref)
    mass_ref[...] = mass_ref[...] * tab_ref[16:80].reshape(mass_ref.shape)

    groups = ((0, 4),) + tuple((u, u + 1) for u in range(4, 13))

    def plan(g):
        lo, hi = groups[g]
        n = hi - lo
        sends = [
            (sj.at[g, 1, 0:n], rj.at[g, 0, 0:n], right, has_right),
            (sj.at[g, 0, 0:n], rj.at[g, 1, 0:n], left, has_left),
            (si.at[g, 1, 0:n], ri.at[g, 0, 0:n], up, has_up),
            (si.at[g, 0, 0:n], ri.at[g, 1, 0:n], down, has_down),
            (sd.at[g, 0, 0:n], rd.at[g, 0, 0:n], up_right, has_up & has_right),
            (sd.at[g, 1, 0:n], rd.at[g, 1, 0:n], up_left, has_up & has_left),
            (sd.at[g, 2, 0:n], rd.at[g, 2, 0:n], down_right, has_down & has_right),
            (sd.at[g, 3, 0:n], rd.at[g, 3, 0:n], down_left, has_down & has_left),
        ]
        copies = [
            pltpu.make_async_remote_copy(
                s, d, ssem.at[g, k], rsem.at[g, k], device_id=(t,), device_id_type=pl.DeviceIdType.MESH
            )
            for k, (s, d, t, _) in enumerate(sends)
        ]
        recv_has = [has_left, has_right, has_down, has_up,
                    has_down & has_left, has_down & has_right, has_up & has_left, has_up & has_right]
        targets = [
            xs.at[lo:hi, :, 0], xs.at[lo:hi, :, 7], xs.at[lo:hi, 0], xs.at[lo:hi, 7],
            xs.at[lo:hi, 0, 0], xs.at[lo:hi, 0, 7], xs.at[lo:hi, 7, 0], xs.at[lo:hi, 7, 7],
        ]
        return sends, copies, recv_has, targets

    def start_group(g):
        prep_group(g)
        launch_group(g)

    def prep_group(g):
        lo, hi = groups[g]
        n = hi - lo
        for u in range(lo, hi):
            xs[u] = z_assemble(xs[u])
        sj[g, 0, 0:n] = xs[lo:hi, :, 0]
        sj[g, 1, 0:n] = xs[lo:hi, :, 7]
        si[g, 0, 0:n] = xs[lo:hi, 0]
        si[g, 1, 0:n] = xs[lo:hi, 7]
        sd[g, 0, 0:n] = xs[lo:hi, 7, 7]
        sd[g, 1, 0:n] = xs[lo:hi, 7, 0]
        sd[g, 2, 0:n] = xs[lo:hi, 0, 7]
        sd[g, 3, 0:n] = xs[lo:hi, 0, 0]

    def launch_group(g):
        sends, copies, _, _ = plan(g)
        for (_, _, _, has), c in zip(sends, copies):
            @pl.when(has)
            def _():
                c.start()

    def finish_group(g):
        sends, copies, recv_has, targets = plan(g)
        for (_, _, _, has), c in zip(sends, copies):
            @pl.when(has)
            def _():
                c.wait_send()
        for k in range(8):
            @pl.when(recv_has[k])
            def _():
                copies[k].wait_recv()
                targets[k][...] = targets[k][...] + sends[k][1][...]

    def flow():
        return (vel_ref[0], vel_ref[1], vel_ref[2])

    xs[0] = mass_ref[...]
    for f in range(3):
        xs[1 + f] = adj_ref[f]
    prep_group(0)
    pl.semaphore_wait(barrier, 8)
    launch_group(0)
    for f in range(3):
        sort_in(fld_in.at[f], fld_ref.at[f])
        sort_in(vel_in.at[f], vel_ref.at[f])
    for f in range(3):
        xs[4 + f] = forward_terms(fld_ref[f], flow(), mass_ref[...], kap_ref[f], tab_ref)
        start_group(1 + f)
    finish_group(0)
    ms_ref[...] = xs[0]
    for f in range(3):
        gathered = xs[1 + f] / ms_ref[...]
        a1 = adj_ref[f] + time_step * adjoint_terms(gathered, flow(), mass_ref[...], kap_ref[f], tab_ref)
        a1_ref[f] = a1
        xs[7 + f] = a1 / ms_ref[...]
        start_group(4 + f)
    for f in range(3):
        finish_group(1 + f)
        f1 = fld_ref[f] + time_step * xs[4 + f] / ms_ref[...]
        f1_ref[f] = f1
        xs[10 + f] = forward_terms(f1, flow(), mass_ref[...], kap_ref[f], tab_ref)
        start_group(7 + f)
    for f in range(3):
        finish_group(4 + f)
        out_a_ref[f] = a1_ref[f] + time_step * adjoint_terms(xs[7 + f], flow(), mass_ref[...], kap_ref[f], tab_ref)
        out_a_in[f] = out_a_ref[f].reshape(512, 128)
    for f in range(3):
        finish_group(7 + f)
        out_f_ref[f] = f1_ref[f] + time_step * xs[10 + f] / ms_ref[...]
        out_f_in[f] = out_f_ref[f].reshape(512, 128)


def unsort_kernel(num_ref, f_ref, a_ref, out_f, out_a):
    count = num_ref.shape[1]
    height = lax.rem(num_ref[...], count)
    p_out = (lax.broadcasted_iota(jnp.int32, (count, count), 0) == height).astype(jnp.bfloat16)
    for f in range(f_ref.shape[0]):
        out_f[f] = permute(f_ref[f], p_out, False)
        out_a[f] = permute(a_ref[f], p_out, False)


def unsort(numbering, moments, sensitivities):
    vmem = pl.BlockSpec(memory_space=pltpu.VMEM)
    shape = jax.ShapeDtypeStruct(moments.shape, jnp.float32)
    return pl.pallas_call(
        unsort_kernel,
        out_shape=(shape, shape),
        in_specs=[vmem, vmem, vmem],
        out_specs=(vmem, vmem),
    )(numbering, moments, sensitivities)


def fused(fields, adjoint, flow, mass, table, numbering, kappa, ndev, cols):
    cube = (8, 8, 8, 128)
    f32 = jnp.float32
    units = 13
    vmem = pl.BlockSpec(memory_space=pltpu.VMEM)
    smem = pl.BlockSpec(memory_space=pltpu.SMEM)
    scratch = [
        pltpu.VMEM((3,) + cube, f32),
        pltpu.VMEM((3,) + cube, f32),
        pltpu.VMEM((3,) + cube, f32),
        pltpu.VMEM(cube, f32),
        pltpu.VMEM((3,) + cube, f32),
        pltpu.VMEM((3,) + cube, f32),
        pltpu.VMEM(cube, f32),
        pltpu.VMEM((3,) + cube, f32),
        pltpu.VMEM((3,) + cube, f32),
        pltpu.VMEM((units,) + cube, f32),
    ]
    groups = 10
    for _ in range(4):
        scratch.append(pltpu.VMEM((groups, 2, 4, 8, 8, 128), f32))
    for _ in range(2):
        scratch.append(pltpu.VMEM((groups, 4, 4, 8, 128), f32))
    scratch += [pltpu.SemaphoreType.DMA((groups, 8)), pltpu.SemaphoreType.DMA((groups, 8))]
    shape = fields.shape
    return pl.pallas_call(
        functools.partial(kernel, ndev, cols),
        out_shape=(jax.ShapeDtypeStruct(shape, f32), jax.ShapeDtypeStruct(shape, f32)),
        in_specs=[vmem, vmem, vmem, vmem, vmem, vmem, smem],
        out_specs=(vmem, vmem),
        scratch_shapes=scratch,
        compiler_params=pltpu.CompilerParams(
            collective_id=0, has_side_effects=True, vmem_limit_bytes=60 * 1024 * 1024
        ),
    )(fields, adjoint, flow, mass, table, numbering, kappa)


def shards(moment_fields, adjoint_fields, velocity, mass_weights, diffusivity, numbering):
    ndev = lax.axis_size("elem")
    cols = ndev // DA
    table = jnp.asarray(shift_tables())
    row_numbers = numbering.reshape(1, -1)
    moments, sensitivities = fused(
        moment_fields, adjoint_fields, velocity, mass_weights, table,
        row_numbers, diffusivity, ndev, cols,
    )
    return unsort(row_numbers, moments, sensitivities)


def solution(mesh):
    in_specs = (
        P(None, None, "elem"),
        P(None, None, "elem"),
        P(None, None, "elem"),
        P(None, "elem"),
        P(),
        P("elem"),
    )
    out_specs = (P(None, None, "elem"), P(None, None, "elem"))
    return jax.shard_map(shards, mesh=mesh, in_specs=in_specs, out_specs=out_specs, check_vma=False)
```

```python
import functools

import jax
import jax.numpy as jnp
import numpy as np
from jax import lax
from jax.experimental import pallas as pl
from jax.experimental.pallas import tpu as pltpu
from jax.sharding import PartitionSpec as P

DA = 4

time_step = 0.001


def gll_tables():
    points = [
        -1.0,
        -0.8717401485096066,
        -0.5917001814331423,
        -0.2092992179024789,
        0.2092992179024789,
        0.5917001814331423,
        0.8717401485096066,
        1.0,
    ]
    weights = [
        0.03571428571428571,
        0.21070422714350603,
        0.3411226924835044,
        0.4124587946587038,
        0.4124587946587038,
        0.3411226924835044,
        0.21070422714350603,
        0.03571428571428571,
    ]
    barycentric = []
    for left_index in range(8):
        product = 1.0
        for right_index in range(8):
            if right_index != left_index:
                product = product * (points[left_index] - points[right_index])
        barycentric.append(1.0 / product)
    derivative = np.zeros((8, 8))
    for left_index in range(8):
        row_total = 0.0
        for right_index in range(8):
            if left_index != right_index:
                entry = (
                    barycentric[right_index]
                    / barycentric[left_index]
                    / (points[left_index] - points[right_index])
                )
                derivative[left_index, right_index] = entry
                row_total = row_total + entry
        derivative[left_index, left_index] = -row_total
    return derivative.astype(np.float32), np.asarray(weights, dtype=np.float32)


DM, WEIGHTS = gll_tables()
DMC = [[float(DM[p, q]) for q in range(8)] for p in range(8)]


def shift_tables():
    fwd = np.zeros((8, 8, 128), np.float32)
    bwd = np.zeros((8, 8, 128), np.float32)
    for s in range(8):
        for p in range(8):
            fwd[s, p, :] = DM[p, (p - s) % 8]
            bwd[s, p, :] = DM[(p - s) % 8, p]
    cube = (WEIGHTS[:, None, None] * WEIGHTS[None, :, None]) * WEIGHTS[None, None, :]
    wrows = np.broadcast_to(cube.reshape(64, 8, 1), (64, 8, 128)).astype(np.float32)
    return np.concatenate([fwd, bwd, wrows], axis=0)


def along_major(v, axis, transpose):
    parts = []
    for p in range(8):
        acc = None
        for q in range(8):
            c = DMC[q][p] if transpose else DMC[p][q]
            term = c * (v[q] if axis == 0 else v[:, q])
            acc = term if acc is None else acc + term
        parts.append(acc)
    return jnp.stack(parts, axis=axis)


def along_sublane(v, tab_ref, base):
    acc = None
    for s in range(8):
        rolled = v if s == 0 else pltpu.roll(v, s, 2)
        term = tab_ref[base + s] * rolled
        acc = term if acc is None else acc + term
    return acc


def gradients(v, tab_ref):
    return (
        along_major(v, 0, False),
        along_major(v, 1, False),
        along_sublane(v, tab_ref, 0),
    )


def transposed(v, tab_ref, direction):
    if direction == 0:
        return along_major(v, 0, True)
    if direction == 1:
        return along_major(v, 1, True)
    return along_sublane(v, tab_ref, 8)


def forward_terms(q, flow, mass, kappa, tab_ref):
    g = gradients(q, tab_ref)
    advect = flow[0] * g[0] + flow[1] * g[1] + flow[2] * g[2]
    diffuse = transposed(mass * g[0], tab_ref, 0)
    diffuse = diffuse + transposed(mass * g[1], tab_ref, 1)
    diffuse = diffuse + transposed(mass * g[2], tab_ref, 2)
    return -(mass * advect) - kappa * diffuse


def adjoint_terms(q, flow, mass, kappa, tab_ref):
    g = gradients(q, tab_ref)
    summed = transposed(mass * (flow[0] * q + kappa * g[0]), tab_ref, 0)
    summed = summed + transposed(mass * (flow[1] * q + kappa * g[1]), tab_ref, 1)
    summed = summed + transposed(mass * (flow[2] * q + kappa * g[2]), tab_ref, 2)
    return -summed


def z_assemble(v):
    shape = v.shape
    sub = lax.broadcasted_iota(jnp.int32, shape, 2)
    lane = lax.broadcasted_iota(jnp.int32, shape, 3)
    below = pltpu.roll(pltpu.roll(v, 1, 2), 1, 3)
    above = pltpu.roll(pltpu.roll(v, 7, 2), 127, 3)
    zero = jnp.zeros_like(v)
    v = v + jnp.where((sub == 0) & (lane > 0), below, zero)
    return v + jnp.where((sub == 7) & (lane < 127), above, zero)


def permute(x, pm, transpose):
    bf = jnp.bfloat16
    f32 = jnp.float32
    dims = (((1,), (1,) if transpose else (0,)), ((), ()))

    def dot(a):
        return lax.dot_general(a, pm, dims, preferred_element_type=f32)

    x1 = x.astype(bf)
    r1 = x - x1.astype(f32)
    x2 = r1.astype(bf)
    x3 = (r1 - x2.astype(f32)).astype(bf)
    return dot(x1) + dot(x2) + dot(x3)


def kernel(
    ndev,
    cols,
    fld_in,
    adj_in,
    vel_in,
    mass_in,
    tab_ref,
    num_ref,
    kap_ref,
    out_f_in,
    out_a_in,
    fld_ref,
    adj_ref,
    vel_ref,
    mass_ref,
    out_f_ref,
    out_a_ref,
    ms_ref,
    f1_ref,
    a1_ref,
    xs,
    sj,
    rj,
    si,
    ri,
    sd,
    rd,
    ssem,
    rsem,
):
    me = lax.axis_index("elem")
    column = (me + cols // 2) % ndev
    place = column % cols
    row = column // cols
    right = (me + 1) % ndev
    left = (me + ndev - 1) % ndev
    up = (me + cols) % ndev
    down = (me + ndev - cols) % ndev
    has_right = place < cols - 1
    has_left = place > 0
    has_up = row < DA - 1
    has_down = row > 0

    up_right = (me + cols + 1) % ndev
    up_left = (me + cols + ndev - 1) % ndev
    down_right = (me + 2 * ndev - cols + 1) % ndev
    down_left = (me + 2 * ndev - cols - 1) % ndev

    barrier = pltpu.get_barrier_semaphore()
    for nb in (left, right, up, down, up_right, up_left, down_right, down_left):
        pl.semaphore_signal(barrier, inc=1, device_id=(nb,), device_id_type=pl.DeviceIdType.MESH)

    count = num_ref.shape[1]
    height = lax.rem(num_ref[...], count)
    p_out = (lax.broadcasted_iota(jnp.int32, (count, count), 0) == height).astype(jnp.bfloat16)

    def sort_in(src_ref, dst_ref):
        dst_ref[...] = permute(src_ref[...], p_out, True).reshape(dst_ref.shape)

    for f in range(3):
        sort_in(adj_in.at[f], adj_ref.at[f])
    sort_in(mass_in, mass_ref)
    mass_ref[...] = mass_ref[...] * tab_ref[16:80].reshape(mass_ref.shape)

    groups = ((0, 4),) + tuple((u, u + 1) for u in range(4, 13))

    def plan(g):
        lo, hi = groups[g]
        n = hi - lo
        sends = [
            (sj.at[g, 1, 0:n], rj.at[g, 0, 0:n], right, has_right),
            (sj.at[g, 0, 0:n], rj.at[g, 1, 0:n], left, has_left),
            (si.at[g, 1, 0:n], ri.at[g, 0, 0:n], up, has_up),
            (si.at[g, 0, 0:n], ri.at[g, 1, 0:n], down, has_down),
            (sd.at[g, 0, 0:n], rd.at[g, 0, 0:n], up_right, has_up & has_right),
            (sd.at[g, 1, 0:n], rd.at[g, 1, 0:n], up_left, has_up & has_left),
            (sd.at[g, 2, 0:n], rd.at[g, 2, 0:n], down_right, has_down & has_right),
            (sd.at[g, 3, 0:n], rd.at[g, 3, 0:n], down_left, has_down & has_left),
        ]
        copies = [
            pltpu.make_async_remote_copy(
                s, d, ssem.at[g, k], rsem.at[g, k], device_id=(t,), device_id_type=pl.DeviceIdType.MESH
            )
            for k, (s, d, t, _) in enumerate(sends)
        ]
        recv_has = [has_left, has_right, has_down, has_up,
                    has_down & has_left, has_down & has_right, has_up & has_left, has_up & has_right]
        targets = [
            xs.at[lo:hi, :, 0], xs.at[lo:hi, :, 7], xs.at[lo:hi, 0], xs.at[lo:hi, 7],
            xs.at[lo:hi, 0, 0], xs.at[lo:hi, 0, 7], xs.at[lo:hi, 7, 0], xs.at[lo:hi, 7, 7],
        ]
        return sends, copies, recv_has, targets

    def start_group(g):
        prep_group(g)
        launch_group(g)

    def prep_group(g):
        lo, hi = groups[g]
        n = hi - lo
        for u in range(lo, hi):
            xs[u] = z_assemble(xs[u])
        sj[g, 0, 0:n] = xs[lo:hi, :, 0]
        sj[g, 1, 0:n] = xs[lo:hi, :, 7]
        si[g, 0, 0:n] = xs[lo:hi, 0]
        si[g, 1, 0:n] = xs[lo:hi, 7]
        sd[g, 0, 0:n] = xs[lo:hi, 7, 7]
        sd[g, 1, 0:n] = xs[lo:hi, 7, 0]
        sd[g, 2, 0:n] = xs[lo:hi, 0, 7]
        sd[g, 3, 0:n] = xs[lo:hi, 0, 0]

    def launch_group(g):
        sends, copies, _, _ = plan(g)
        for (_, _, _, has), c in zip(sends, copies):
            @pl.when(has)
            def _():
                c.start()

    def finish_group(g):
        sends, copies, recv_has, targets = plan(g)
        for (_, _, _, has), c in zip(sends, copies):
            @pl.when(has)
            def _():
                c.wait_send()
        for k in range(8):
            @pl.when(recv_has[k])
            def _():
                copies[k].wait_recv()
                targets[k][...] = targets[k][...] + sends[k][1][...]

    def flow():
        return (vel_ref[0], vel_ref[1], vel_ref[2])

    xs[0] = mass_ref[...]
    for f in range(3):
        xs[1 + f] = adj_ref[f]
    prep_group(0)
    pl.semaphore_wait(barrier, 8)
    launch_group(0)
    for f in range(3):
        sort_in(fld_in.at[f], fld_ref.at[f])
        sort_in(vel_in.at[f], vel_ref.at[f])
    for f in range(3):
        xs[4 + f] = forward_terms(fld_ref[f], flow(), mass_ref[...], kap_ref[f], tab_ref)
        start_group(1 + f)
    finish_group(0)
    ms_ref[...] = xs[0]
    for f in range(3):
        gathered = xs[1 + f] / ms_ref[...]
        a1 = adj_ref[f] + time_step * adjoint_terms(gathered, flow(), mass_ref[...], kap_ref[f], tab_ref)
        a1_ref[f] = a1
        xs[7 + f] = a1 / ms_ref[...]
        start_group(4 + f)
    for f in range(3):
        finish_group(1 + f)
        f1 = fld_ref[f] + time_step * xs[4 + f] / ms_ref[...]
        f1_ref[f] = f1
        xs[10 + f] = forward_terms(f1, flow(), mass_ref[...], kap_ref[f], tab_ref)
        start_group(7 + f)
    for f in range(3):
        finish_group(4 + f)
        out_a_ref[f] = a1_ref[f] + time_step * adjoint_terms(xs[7 + f], flow(), mass_ref[...], kap_ref[f], tab_ref)
        out_a_in[f] = out_a_ref[f].reshape(512, 128)
    for f in range(3):
        finish_group(7 + f)
        out_f_ref[f] = f1_ref[f] + time_step * xs[10 + f] / ms_ref[...]
        out_f_in[f] = out_f_ref[f].reshape(512, 128)


def unsort_kernel(num_ref, f_ref, a_ref, out_f, out_a):
    count = num_ref.shape[1]
    height = lax.rem(num_ref[...], count)
    p_out = (lax.broadcasted_iota(jnp.int32, (count, count), 0) == height).astype(jnp.bfloat16)
    out_f[0] = permute(f_ref[0], p_out, False)
    out_a[0] = permute(a_ref[0], p_out, False)


def unsort(numbering, moments, sensitivities):
    count, nodes, width = moments.shape
    block = pl.BlockSpec((1, nodes, width), lambda f: (f, 0, 0))
    shape = jax.ShapeDtypeStruct(moments.shape, jnp.float32)
    return pl.pallas_call(
        unsort_kernel,
        grid=(count,),
        out_shape=(shape, shape),
        in_specs=[pl.BlockSpec(numbering.shape, lambda f: (0, 0)), block, block],
        out_specs=(block, block),
    )(numbering, moments, sensitivities)


def fused(fields, adjoint, flow, mass, table, numbering, kappa, ndev, cols):
    cube = (8, 8, 8, 128)
    f32 = jnp.float32
    units = 13
    vmem = pl.BlockSpec(memory_space=pltpu.VMEM)
    smem = pl.BlockSpec(memory_space=pltpu.SMEM)
    scratch = [
        pltpu.VMEM((3,) + cube, f32),
        pltpu.VMEM((3,) + cube, f32),
        pltpu.VMEM((3,) + cube, f32),
        pltpu.VMEM(cube, f32),
        pltpu.VMEM((3,) + cube, f32),
        pltpu.VMEM((3,) + cube, f32),
        pltpu.VMEM(cube, f32),
        pltpu.VMEM((3,) + cube, f32),
        pltpu.VMEM((3,) + cube, f32),
        pltpu.VMEM((units,) + cube, f32),
    ]
    groups = 10
    for _ in range(4):
        scratch.append(pltpu.VMEM((groups, 2, 4, 8, 8, 128), f32))
    for _ in range(2):
        scratch.append(pltpu.VMEM((groups, 4, 4, 8, 128), f32))
    scratch += [pltpu.SemaphoreType.DMA((groups, 8)), pltpu.SemaphoreType.DMA((groups, 8))]
    shape = fields.shape
    return pl.pallas_call(
        functools.partial(kernel, ndev, cols),
        out_shape=(jax.ShapeDtypeStruct(shape, f32), jax.ShapeDtypeStruct(shape, f32)),
        in_specs=[vmem, vmem, vmem, vmem, vmem, vmem, smem],
        out_specs=(vmem, vmem),
        scratch_shapes=scratch,
        compiler_params=pltpu.CompilerParams(
            collective_id=0, has_side_effects=True, vmem_limit_bytes=60 * 1024 * 1024
        ),
    )(fields, adjoint, flow, mass, table, numbering, kappa)


def shards(moment_fields, adjoint_fields, velocity, mass_weights, diffusivity, numbering):
    ndev = lax.axis_size("elem")
    cols = ndev // DA
    table = jnp.asarray(shift_tables())
    row_numbers = numbering.reshape(1, -1)
    moments, sensitivities = fused(
        moment_fields, adjoint_fields, velocity, mass_weights, table,
        row_numbers, diffusivity, ndev, cols,
    )
    return unsort(row_numbers, moments, sensitivities)


def solution(mesh):
    in_specs = (
        P(None, None, "elem"),
        P(None, None, "elem"),
        P(None, None, "elem"),
        P(None, "elem"),
        P(),
        P("elem"),
    )
    out_specs = (P(None, None, "elem"), P(None, None, "elem"))
    return jax.shard_map(shards, mesh=mesh, in_specs=in_specs, out_specs=out_specs, check_vma=False)
```

```python
import functools

import jax
import jax.numpy as jnp
import numpy as np
from jax import lax
from jax.experimental import pallas as pl
from jax.experimental.pallas import tpu as pltpu
from jax.sharding import PartitionSpec as P

DA = 4

time_step = 0.001


def gll_tables():
    points = [
        -1.0,
        -0.8717401485096066,
        -0.5917001814331423,
        -0.2092992179024789,
        0.2092992179024789,
        0.5917001814331423,
        0.8717401485096066,
        1.0,
    ]
    weights = [
        0.03571428571428571,
        0.21070422714350603,
        0.3411226924835044,
        0.4124587946587038,
        0.4124587946587038,
        0.3411226924835044,
        0.21070422714350603,
        0.03571428571428571,
    ]
    barycentric = []
    for left_index in range(8):
        product = 1.0
        for right_index in range(8):
            if right_index != left_index:
                product = product * (points[left_index] - points[right_index])
        barycentric.append(1.0 / product)
    derivative = np.zeros((8, 8))
    for left_index in range(8):
        row_total = 0.0
        for right_index in range(8):
            if left_index != right_index:
                entry = (
                    barycentric[right_index]
                    / barycentric[left_index]
                    / (points[left_index] - points[right_index])
                )
                derivative[left_index, right_index] = entry
                row_total = row_total + entry
        derivative[left_index, left_index] = -row_total
    return derivative.astype(np.float32), np.asarray(weights, dtype=np.float32)


DM, WEIGHTS = gll_tables()
DMC = [[float(DM[p, q]) for q in range(8)] for p in range(8)]


def shift_tables():
    fwd = np.zeros((8, 8, 128), np.float32)
    bwd = np.zeros((8, 8, 128), np.float32)
    for s in range(8):
        for p in range(8):
            fwd[s, p, :] = DM[p, (p - s) % 8]
            bwd[s, p, :] = DM[(p - s) % 8, p]
    cube = (WEIGHTS[:, None, None] * WEIGHTS[None, :, None]) * WEIGHTS[None, None, :]
    wrows = np.broadcast_to(cube.reshape(64, 8, 1), (64, 8, 128)).astype(np.float32)
    return np.concatenate([fwd, bwd, wrows], axis=0)


def along_major(v, axis, transpose):
    parts = []
    for p in range(8):
        acc = None
        for q in range(8):
            c = DMC[q][p] if transpose else DMC[p][q]
            term = c * (v[q] if axis == 0 else v[:, q])
            acc = term if acc is None else acc + term
        parts.append(acc)
    return jnp.stack(parts, axis=axis)


def along_sublane(v, tab_ref, base):
    acc = None
    for s in range(8):
        rolled = v if s == 0 else pltpu.roll(v, s, 2)
        term = tab_ref[base + s] * rolled
        acc = term if acc is None else acc + term
    return acc


def gradients(v, tab_ref):
    return (
        along_major(v, 0, False),
        along_major(v, 1, False),
        along_sublane(v, tab_ref, 0),
    )


def transposed(v, tab_ref, direction):
    if direction == 0:
        return along_major(v, 0, True)
    if direction == 1:
        return along_major(v, 1, True)
    return along_sublane(v, tab_ref, 8)


def forward_terms(q, flow, mass, kappa, tab_ref):
    g = gradients(q, tab_ref)
    advect = flow[0] * g[0] + flow[1] * g[1] + flow[2] * g[2]
    diffuse = transposed(mass * g[0], tab_ref, 0)
    diffuse = diffuse + transposed(mass * g[1], tab_ref, 1)
    diffuse = diffuse + transposed(mass * g[2], tab_ref, 2)
    return -(mass * advect) - kappa * diffuse


def adjoint_terms(q, flow, mass, kappa, tab_ref):
    g = gradients(q, tab_ref)
    summed = transposed(mass * (flow[0] * q + kappa * g[0]), tab_ref, 0)
    summed = summed + transposed(mass * (flow[1] * q + kappa * g[1]), tab_ref, 1)
    summed = summed + transposed(mass * (flow[2] * q + kappa * g[2]), tab_ref, 2)
    return -summed


def z_assemble(v):
    shape = v.shape
    sub = lax.broadcasted_iota(jnp.int32, shape, 2)
    lane = lax.broadcasted_iota(jnp.int32, shape, 3)
    below = pltpu.roll(pltpu.roll(v, 1, 2), 1, 3)
    above = pltpu.roll(pltpu.roll(v, 7, 2), 127, 3)
    zero = jnp.zeros_like(v)
    v = v + jnp.where((sub == 0) & (lane > 0), below, zero)
    return v + jnp.where((sub == 7) & (lane < 127), above, zero)


def permute(x, pm, transpose):
    bf = jnp.bfloat16
    f32 = jnp.float32
    dims = (((1,), (1,) if transpose else (0,)), ((), ()))

    def dot(a):
        return lax.dot_general(a, pm, dims, preferred_element_type=f32)

    x1 = x.astype(bf)
    r1 = x - x1.astype(f32)
    x2 = r1.astype(bf)
    x3 = (r1 - x2.astype(f32)).astype(bf)
    return dot(x1) + dot(x2) + dot(x3)


def kernel(
    ndev,
    cols,
    fld_in,
    adj_in,
    vel_in,
    mass_in,
    tab_ref,
    num_ref,
    kap_ref,
    out_f_in,
    out_a_in,
    fld_ref,
    adj_ref,
    vel_ref,
    mass_ref,
    out_f_ref,
    out_a_ref,
    ms_ref,
    f1_ref,
    a1_ref,
    xs,
    sj,
    rj,
    si,
    ri,
    sd,
    rd,
    ssem,
    rsem,
):
    me = lax.axis_index("elem")
    column = (me + cols // 2) % ndev
    place = column % cols
    row = column // cols
    right = (me + 1) % ndev
    left = (me + ndev - 1) % ndev
    up = (me + cols) % ndev
    down = (me + ndev - cols) % ndev
    has_right = place < cols - 1
    has_left = place > 0
    has_up = row < DA - 1
    has_down = row > 0

    up_right = (me + cols + 1) % ndev
    up_left = (me + cols + ndev - 1) % ndev
    down_right = (me + 2 * ndev - cols + 1) % ndev
    down_left = (me + 2 * ndev - cols - 1) % ndev

    barrier = pltpu.get_barrier_semaphore()
    for nb in (left, right, up, down, up_right, up_left, down_right, down_left):
        pl.semaphore_signal(barrier, inc=1, device_id=(nb,), device_id_type=pl.DeviceIdType.MESH)

    count = num_ref.shape[1]
    height = lax.rem(num_ref[...], count)
    p_out = (lax.broadcasted_iota(jnp.int32, (count, count), 0) == height).astype(jnp.bfloat16)

    def sort_in(src_ref, dst_ref):
        dst_ref[...] = permute(src_ref[...], p_out, True).reshape(dst_ref.shape)

    for f in range(3):
        sort_in(adj_in.at[f], adj_ref.at[f])
    sort_in(mass_in, mass_ref)
    mass_ref[...] = mass_ref[...] * tab_ref[16:80].reshape(mass_ref.shape)

    groups = ((0, 4),) + tuple((u, u + 1) for u in range(4, 13))

    def plan(g):
        lo, hi = groups[g]
        n = hi - lo
        sends = [
            (sj.at[g, 1, 0:n], rj.at[g, 0, 0:n], right, has_right),
            (sj.at[g, 0, 0:n], rj.at[g, 1, 0:n], left, has_left),
            (si.at[g, 1, 0:n], ri.at[g, 0, 0:n], up, has_up),
            (si.at[g, 0, 0:n], ri.at[g, 1, 0:n], down, has_down),
            (sd.at[g, 0, 0:n], rd.at[g, 0, 0:n], up_right, has_up & has_right),
            (sd.at[g, 1, 0:n], rd.at[g, 1, 0:n], up_left, has_up & has_left),
            (sd.at[g, 2, 0:n], rd.at[g, 2, 0:n], down_right, has_down & has_right),
            (sd.at[g, 3, 0:n], rd.at[g, 3, 0:n], down_left, has_down & has_left),
        ]
        copies = [
            pltpu.make_async_remote_copy(
                s, d, ssem.at[g, k], rsem.at[g, k], device_id=(t,), device_id_type=pl.DeviceIdType.MESH
            )
            for k, (s, d, t, _) in enumerate(sends)
        ]
        recv_has = [has_left, has_right, has_down, has_up,
                    has_down & has_left, has_down & has_right, has_up & has_left, has_up & has_right]
        targets = [
            xs.at[lo:hi, :, 0], xs.at[lo:hi, :, 7], xs.at[lo:hi, 0], xs.at[lo:hi, 7],
            xs.at[lo:hi, 0, 0], xs.at[lo:hi, 0, 7], xs.at[lo:hi, 7, 0], xs.at[lo:hi, 7, 7],
        ]
        return sends, copies, recv_has, targets

    def start_group(g):
        prep_group(g)
        launch_group(g)

    def prep_group(g):
        lo, hi = groups[g]
        n = hi - lo
        for u in range(lo, hi):
            xs[u] = z_assemble(xs[u])
        sj[g, 0, 0:n] = xs[lo:hi, :, 0]
        sj[g, 1, 0:n] = xs[lo:hi, :, 7]
        si[g, 0, 0:n] = xs[lo:hi, 0]
        si[g, 1, 0:n] = xs[lo:hi, 7]
        sd[g, 0, 0:n] = xs[lo:hi, 7, 7]
        sd[g, 1, 0:n] = xs[lo:hi, 7, 0]
        sd[g, 2, 0:n] = xs[lo:hi, 0, 7]
        sd[g, 3, 0:n] = xs[lo:hi, 0, 0]

    def launch_group(g):
        sends, copies, _, _ = plan(g)
        for (_, _, _, has), c in zip(sends, copies):
            @pl.when(has)
            def _():
                c.start()

    def finish_group(g):
        sends, copies, recv_has, targets = plan(g)
        for (_, _, _, has), c in zip(sends, copies):
            @pl.when(has)
            def _():
                c.wait_send()
        for k in range(8):
            @pl.when(recv_has[k])
            def _():
                copies[k].wait_recv()
                targets[k][...] = targets[k][...] + sends[k][1][...]

    def flow():
        return (vel_ref[0], vel_ref[1], vel_ref[2])

    xs[0] = mass_ref[...]
    for f in range(3):
        xs[1 + f] = adj_ref[f]
    prep_group(0)
    pl.semaphore_wait(barrier, 8)
    launch_group(0)
    for f in range(3):
        sort_in(fld_in.at[f], fld_ref.at[f])
        sort_in(vel_in.at[f], vel_ref.at[f])
    for f in range(3):
        xs[4 + f] = forward_terms(fld_ref[f], flow(), mass_ref[...], kap_ref[f], tab_ref)
        start_group(1 + f)
    finish_group(0)
    ms_ref[...] = xs[0]
    for f in range(3):
        gathered = xs[1 + f] / ms_ref[...]
        a1 = adj_ref[f] + time_step * adjoint_terms(gathered, flow(), mass_ref[...], kap_ref[f], tab_ref)
        a1_ref[f] = a1
        xs[7 + f] = a1 / ms_ref[...]
        start_group(4 + f)
    for f in range(3):
        finish_group(1 + f)
        f1 = fld_ref[f] + time_step * xs[4 + f] / ms_ref[...]
        f1_ref[f] = f1
        xs[10 + f] = forward_terms(f1, flow(), mass_ref[...], kap_ref[f], tab_ref)
        start_group(7 + f)
    for f in range(3):
        finish_group(4 + f)
        out_a_ref[f] = a1_ref[f] + time_step * adjoint_terms(xs[7 + f], flow(), mass_ref[...], kap_ref[f], tab_ref)
        out_a_in[f] = out_a_ref[f].reshape(512, 128)
    for f in range(3):
        finish_group(7 + f)
        out_f_ref[f] = f1_ref[f] + time_step * xs[10 + f] / ms_ref[...]
        out_f_in[f] = out_f_ref[f].reshape(512, 128)


def unsort_kernel(num_ref, f_hbm, a_hbm, out_f, out_a, buf_in, buf_out, sem_in, sem_out):
    count = num_ref.shape[1]
    fields = f_hbm.shape[0]
    srcs = [r.at[f] for f in range(fields) for r in (f_hbm, a_hbm)]
    dsts = [r.at[f] for f in range(fields) for r in (out_f, out_a)]
    loads = [pltpu.make_async_copy(s, buf_in.at[i], sem_in.at[i]) for i, s in enumerate(srcs)]
    for c in loads:
        c.start()
    height = lax.rem(num_ref[...], count)
    p_out = (lax.broadcasted_iota(jnp.int32, (count, count), 0) == height).astype(jnp.bfloat16)
    stores = []
    for i, c in enumerate(loads):
        c.wait()
        buf_out[i] = permute(buf_in[i], p_out, False)
        st = pltpu.make_async_copy(buf_out.at[i], dsts[i], sem_out.at[i])
        st.start()
        stores.append(st)
    for st in stores:
        st.wait()


def unsort(numbering, moments, sensitivities):
    vmem = pl.BlockSpec(memory_space=pltpu.VMEM)
    hbm = pl.BlockSpec(memory_space=pl.ANY)
    slabs = 2 * moments.shape[0]
    shape = jax.ShapeDtypeStruct(moments.shape, jnp.float32)
    return pl.pallas_call(
        unsort_kernel,
        out_shape=(shape, shape),
        in_specs=[vmem, hbm, hbm],
        out_specs=(hbm, hbm),
        scratch_shapes=[
            pltpu.VMEM((slabs,) + moments.shape[1:], jnp.float32),
            pltpu.VMEM((slabs,) + moments.shape[1:], jnp.float32),
            pltpu.SemaphoreType.DMA((slabs,)),
            pltpu.SemaphoreType.DMA((slabs,)),
        ],
    )(numbering, moments, sensitivities)


def fused(fields, adjoint, flow, mass, table, numbering, kappa, ndev, cols):
    cube = (8, 8, 8, 128)
    f32 = jnp.float32
    units = 13
    vmem = pl.BlockSpec(memory_space=pltpu.VMEM)
    smem = pl.BlockSpec(memory_space=pltpu.SMEM)
    scratch = [
        pltpu.VMEM((3,) + cube, f32),
        pltpu.VMEM((3,) + cube, f32),
        pltpu.VMEM((3,) + cube, f32),
        pltpu.VMEM(cube, f32),
        pltpu.VMEM((3,) + cube, f32),
        pltpu.VMEM((3,) + cube, f32),
        pltpu.VMEM(cube, f32),
        pltpu.VMEM((3,) + cube, f32),
        pltpu.VMEM((3,) + cube, f32),
        pltpu.VMEM((units,) + cube, f32),
    ]
    groups = 10
    for _ in range(4):
        scratch.append(pltpu.VMEM((groups, 2, 4, 8, 8, 128), f32))
    for _ in range(2):
        scratch.append(pltpu.VMEM((groups, 4, 4, 8, 128), f32))
    scratch += [pltpu.SemaphoreType.DMA((groups, 8)), pltpu.SemaphoreType.DMA((groups, 8))]
    shape = fields.shape
    return pl.pallas_call(
        functools.partial(kernel, ndev, cols),
        out_shape=(jax.ShapeDtypeStruct(shape, f32), jax.ShapeDtypeStruct(shape, f32)),
        in_specs=[vmem, vmem, vmem, vmem, vmem, vmem, smem],
        out_specs=(vmem, vmem),
        scratch_shapes=scratch,
        compiler_params=pltpu.CompilerParams(
            collective_id=0, has_side_effects=True, vmem_limit_bytes=60 * 1024 * 1024
        ),
    )(fields, adjoint, flow, mass, table, numbering, kappa)


def shards(moment_fields, adjoint_fields, velocity, mass_weights, diffusivity, numbering):
    ndev = lax.axis_size("elem")
    cols = ndev // DA
    table = jnp.asarray(shift_tables())
    row_numbers = numbering.reshape(1, -1)
    moments, sensitivities = fused(
        moment_fields, adjoint_fields, velocity, mass_weights, table,
        row_numbers, diffusivity, ndev, cols,
    )
    return unsort(row_numbers, moments, sensitivities)


def solution(mesh):
    in_specs = (
        P(None, None, "elem"),
        P(None, None, "elem"),
        P(None, None, "elem"),
        P(None, "elem"),
        P(),
        P("elem"),
    )
    out_specs = (P(None, None, "elem"), P(None, None, "elem"))
    return jax.shard_map(shards, mesh=mesh, in_specs=in_specs, out_specs=out_specs, check_vma=False)
```

```python
import functools

import jax
import jax.numpy as jnp
import numpy as np
from jax import lax
from jax.experimental import pallas as pl
from jax.experimental.pallas import tpu as pltpu
from jax.sharding import PartitionSpec as P

DA = 4

time_step = 0.001


def gll_tables():
    points = [
        -1.0,
        -0.8717401485096066,
        -0.5917001814331423,
        -0.2092992179024789,
        0.2092992179024789,
        0.5917001814331423,
        0.8717401485096066,
        1.0,
    ]
    weights = [
        0.03571428571428571,
        0.21070422714350603,
        0.3411226924835044,
        0.4124587946587038,
        0.4124587946587038,
        0.3411226924835044,
        0.21070422714350603,
        0.03571428571428571,
    ]
    barycentric = []
    for left_index in range(8):
        product = 1.0
        for right_index in range(8):
            if right_index != left_index:
                product = product * (points[left_index] - points[right_index])
        barycentric.append(1.0 / product)
    derivative = np.zeros((8, 8))
    for left_index in range(8):
        row_total = 0.0
        for right_index in range(8):
            if left_index != right_index:
                entry = (
                    barycentric[right_index]
                    / barycentric[left_index]
                    / (points[left_index] - points[right_index])
                )
                derivative[left_index, right_index] = entry
                row_total = row_total + entry
        derivative[left_index, left_index] = -row_total
    return derivative.astype(np.float32), np.asarray(weights, dtype=np.float32)


DM, WEIGHTS = gll_tables()
DMC = [[float(DM[p, q]) for q in range(8)] for p in range(8)]


def shift_tables():
    fwd = np.zeros((8, 8, 128), np.float32)
    bwd = np.zeros((8, 8, 128), np.float32)
    for s in range(8):
        for p in range(8):
            fwd[s, p, :] = DM[p, (p - s) % 8]
            bwd[s, p, :] = DM[(p - s) % 8, p]
    cube = (WEIGHTS[:, None, None] * WEIGHTS[None, :, None]) * WEIGHTS[None, None, :]
    wrows = np.broadcast_to(cube.reshape(64, 8, 1), (64, 8, 128)).astype(np.float32)
    return np.concatenate([fwd, bwd, wrows], axis=0)


def along_major(v, axis, transpose):
    parts = []
    for p in range(8):
        acc = None
        for q in range(8):
            c = DMC[q][p] if transpose else DMC[p][q]
            term = c * (v[q] if axis == 0 else v[:, q])
            acc = term if acc is None else acc + term
        parts.append(acc)
    return jnp.stack(parts, axis=axis)


def along_sublane(v, tab_ref, base):
    acc = None
    for s in range(8):
        rolled = v if s == 0 else pltpu.roll(v, s, 2)
        term = tab_ref[base + s] * rolled
        acc = term if acc is None else acc + term
    return acc


def gradients(v, tab_ref):
    return (
        along_major(v, 0, False),
        along_major(v, 1, False),
        along_sublane(v, tab_ref, 0),
    )


def transposed(v, tab_ref, direction):
    if direction == 0:
        return along_major(v, 0, True)
    if direction == 1:
        return along_major(v, 1, True)
    return along_sublane(v, tab_ref, 8)


def forward_terms(q, flow, mass, kappa, tab_ref):
    g = gradients(q, tab_ref)
    advect = flow[0] * g[0] + flow[1] * g[1] + flow[2] * g[2]
    diffuse = transposed(mass * g[0], tab_ref, 0)
    diffuse = diffuse + transposed(mass * g[1], tab_ref, 1)
    diffuse = diffuse + transposed(mass * g[2], tab_ref, 2)
    return -(mass * advect) - kappa * diffuse


def adjoint_terms(q, flow, mass, kappa, tab_ref):
    g = gradients(q, tab_ref)
    summed = transposed(mass * (flow[0] * q + kappa * g[0]), tab_ref, 0)
    summed = summed + transposed(mass * (flow[1] * q + kappa * g[1]), tab_ref, 1)
    summed = summed + transposed(mass * (flow[2] * q + kappa * g[2]), tab_ref, 2)
    return -summed


def z_assemble(v):
    shape = v.shape
    sub = lax.broadcasted_iota(jnp.int32, shape, 2)
    lane = lax.broadcasted_iota(jnp.int32, shape, 3)
    below = pltpu.roll(pltpu.roll(v, 1, 2), 1, 3)
    above = pltpu.roll(pltpu.roll(v, 7, 2), 127, 3)
    zero = jnp.zeros_like(v)
    v = v + jnp.where((sub == 0) & (lane > 0), below, zero)
    return v + jnp.where((sub == 7) & (lane < 127), above, zero)


def permute(x, pm, transpose):
    bf = jnp.bfloat16
    f32 = jnp.float32
    dims = (((1,), (1,) if transpose else (0,)), ((), ()))

    def dot(a):
        return lax.dot_general(a, pm, dims, preferred_element_type=f32)

    x1 = x.astype(bf)
    r1 = x - x1.astype(f32)
    x2 = r1.astype(bf)
    x3 = (r1 - x2.astype(f32)).astype(bf)
    return dot(x1) + dot(x2) + dot(x3)


def kernel(
    ndev,
    cols,
    fld_in,
    adj_in,
    vel_in,
    mass_in,
    tab_ref,
    num_ref,
    kap_ref,
    out_f_in,
    out_a_in,
    fld_ref,
    adj_ref,
    vel_ref,
    mass_ref,
    out_f_ref,
    out_a_ref,
    ms_ref,
    f1_ref,
    a1_ref,
    xs,
    sj,
    rj,
    si,
    ri,
    sd,
    rd,
    ssem,
    rsem,
    osem,
):
    me = lax.axis_index("elem")
    column = (me + cols // 2) % ndev
    place = column % cols
    row = column // cols
    right = (me + 1) % ndev
    left = (me + ndev - 1) % ndev
    up = (me + cols) % ndev
    down = (me + ndev - cols) % ndev
    has_right = place < cols - 1
    has_left = place > 0
    has_up = row < DA - 1
    has_down = row > 0

    up_right = (me + cols + 1) % ndev
    up_left = (me + cols + ndev - 1) % ndev
    down_right = (me + 2 * ndev - cols + 1) % ndev
    down_left = (me + 2 * ndev - cols - 1) % ndev

    barrier = pltpu.get_barrier_semaphore()
    for nb in (left, right, up, down, up_right, up_left, down_right, down_left):
        pl.semaphore_signal(barrier, inc=1, device_id=(nb,), device_id_type=pl.DeviceIdType.MESH)

    count = num_ref.shape[1]
    height = lax.rem(num_ref[...], count)
    p_out = (lax.broadcasted_iota(jnp.int32, (count, count), 0) == height).astype(jnp.bfloat16)

    def sort_in(src_ref, dst_ref):
        dst_ref[...] = permute(src_ref[...], p_out, True).reshape(dst_ref.shape)

    for f in range(3):
        sort_in(adj_in.at[f], adj_ref.at[f])
    sort_in(mass_in, mass_ref)
    mass_ref[...] = mass_ref[...] * tab_ref[16:80].reshape(mass_ref.shape)

    groups = ((0, 4),) + tuple((u, u + 1) for u in range(4, 13))

    def plan(g):
        lo, hi = groups[g]
        n = hi - lo
        sends = [
            (sj.at[g, 1, 0:n], rj.at[g, 0, 0:n], right, has_right),
            (sj.at[g, 0, 0:n], rj.at[g, 1, 0:n], left, has_left),
            (si.at[g, 1, 0:n], ri.at[g, 0, 0:n], up, has_up),
            (si.at[g, 0, 0:n], ri.at[g, 1, 0:n], down, has_down),
            (sd.at[g, 0, 0:n], rd.at[g, 0, 0:n], up_right, has_up & has_right),
            (sd.at[g, 1, 0:n], rd.at[g, 1, 0:n], up_left, has_up & has_left),
            (sd.at[g, 2, 0:n], rd.at[g, 2, 0:n], down_right, has_down & has_right),
            (sd.at[g, 3, 0:n], rd.at[g, 3, 0:n], down_left, has_down & has_left),
        ]
        copies = [
            pltpu.make_async_remote_copy(
                s, d, ssem.at[g, k], rsem.at[g, k], device_id=(t,), device_id_type=pl.DeviceIdType.MESH
            )
            for k, (s, d, t, _) in enumerate(sends)
        ]
        recv_has = [has_left, has_right, has_down, has_up,
                    has_down & has_left, has_down & has_right, has_up & has_left, has_up & has_right]
        targets = [
            xs.at[lo:hi, :, 0], xs.at[lo:hi, :, 7], xs.at[lo:hi, 0], xs.at[lo:hi, 7],
            xs.at[lo:hi, 0, 0], xs.at[lo:hi, 0, 7], xs.at[lo:hi, 7, 0], xs.at[lo:hi, 7, 7],
        ]
        return sends, copies, recv_has, targets

    def start_group(g):
        prep_group(g)
        launch_group(g)

    def prep_group(g):
        lo, hi = groups[g]
        n = hi - lo
        for u in range(lo, hi):
            xs[u] = z_assemble(xs[u])
        sj[g, 0, 0:n] = xs[lo:hi, :, 0]
        sj[g, 1, 0:n] = xs[lo:hi, :, 7]
        si[g, 0, 0:n] = xs[lo:hi, 0]
        si[g, 1, 0:n] = xs[lo:hi, 7]
        sd[g, 0, 0:n] = xs[lo:hi, 7, 7]
        sd[g, 1, 0:n] = xs[lo:hi, 7, 0]
        sd[g, 2, 0:n] = xs[lo:hi, 0, 7]
        sd[g, 3, 0:n] = xs[lo:hi, 0, 0]

    def launch_group(g):
        sends, copies, _, _ = plan(g)
        for (_, _, _, has), c in zip(sends, copies):
            @pl.when(has)
            def _():
                c.start()

    def finish_group(g):
        sends, copies, recv_has, targets = plan(g)
        for (_, _, _, has), c in zip(sends, copies):
            @pl.when(has)
            def _():
                c.wait_send()
        for k in range(8):
            @pl.when(recv_has[k])
            def _():
                copies[k].wait_recv()
                targets[k][...] = targets[k][...] + sends[k][1][...]

    def flow():
        return (vel_ref[0], vel_ref[1], vel_ref[2])

    xs[0] = mass_ref[...]
    for f in range(3):
        xs[1 + f] = adj_ref[f]
    prep_group(0)
    pl.semaphore_wait(barrier, 8)
    launch_group(0)
    for f in range(3):
        sort_in(fld_in.at[f], fld_ref.at[f])
        sort_in(vel_in.at[f], vel_ref.at[f])
    for f in range(3):
        xs[4 + f] = forward_terms(fld_ref[f], flow(), mass_ref[...], kap_ref[f], tab_ref)
        start_group(1 + f)
    finish_group(0)
    ms_ref[...] = xs[0]
    for f in range(3):
        gathered = xs[1 + f] / ms_ref[...]
        a1 = adj_ref[f] + time_step * adjoint_terms(gathered, flow(), mass_ref[...], kap_ref[f], tab_ref)
        a1_ref[f] = a1
        xs[7 + f] = a1 / ms_ref[...]
        start_group(4 + f)
    for f in range(3):
        finish_group(1 + f)
        f1 = fld_ref[f] + time_step * xs[4 + f] / ms_ref[...]
        f1_ref[f] = f1
        xs[10 + f] = forward_terms(f1, flow(), mass_ref[...], kap_ref[f], tab_ref)
        start_group(7 + f)
    outs = []
    for f in range(3):
        finish_group(4 + f)
        out_a_ref[f] = a1_ref[f] + time_step * adjoint_terms(xs[7 + f], flow(), mass_ref[...], kap_ref[f], tab_ref)
        outs.append(pltpu.make_async_copy(out_a_ref.at[f], out_a_in.at[f], osem.at[f]))
        outs[-1].start()
    for f in range(3):
        finish_group(7 + f)
        out_f_ref[f] = f1_ref[f] + time_step * xs[10 + f] / ms_ref[...]
        outs.append(pltpu.make_async_copy(out_f_ref.at[f], out_f_in.at[f], osem.at[3 + f]))
        outs[-1].start()
    for c in outs:
        c.wait()


def unsort_kernel(num_ref, f_ref, a_ref, out_f, out_a):
    count = num_ref.shape[1]
    height = lax.rem(num_ref[...], count)
    p_out = (lax.broadcasted_iota(jnp.int32, (count, count), 0) == height).astype(jnp.bfloat16)
    for f in range(f_ref.shape[0]):
        out_f[f] = permute(f_ref[f], p_out, False)
        out_a[f] = permute(a_ref[f], p_out, False)


def unsort(numbering, moments, sensitivities):
    vmem = pl.BlockSpec(memory_space=pltpu.VMEM)
    shape = jax.ShapeDtypeStruct(moments.shape, jnp.float32)
    return pl.pallas_call(
        unsort_kernel,
        out_shape=(shape, shape),
        in_specs=[vmem, vmem, vmem],
        out_specs=(vmem, vmem),
    )(numbering, moments, sensitivities)


def fused(fields, adjoint, flow, mass, table, numbering, kappa, ndev, cols):
    cube = (8, 8, 8, 128)
    f32 = jnp.float32
    units = 13
    vmem = pl.BlockSpec(memory_space=pltpu.VMEM)
    smem = pl.BlockSpec(memory_space=pltpu.SMEM)
    scratch = [
        pltpu.VMEM((3,) + cube, f32),
        pltpu.VMEM((3,) + cube, f32),
        pltpu.VMEM((3,) + cube, f32),
        pltpu.VMEM(cube, f32),
        pltpu.VMEM((3,) + cube, f32),
        pltpu.VMEM((3,) + cube, f32),
        pltpu.VMEM(cube, f32),
        pltpu.VMEM((3,) + cube, f32),
        pltpu.VMEM((3,) + cube, f32),
        pltpu.VMEM((units,) + cube, f32),
    ]
    groups = 10
    for _ in range(4):
        scratch.append(pltpu.VMEM((groups, 2, 4, 8, 8, 128), f32))
    for _ in range(2):
        scratch.append(pltpu.VMEM((groups, 4, 4, 8, 128), f32))
    scratch += [pltpu.SemaphoreType.DMA((groups, 8)), pltpu.SemaphoreType.DMA((groups, 8))]
    scratch.append(pltpu.SemaphoreType.DMA((6,)))
    shape = fields.shape
    return pl.pallas_call(
        functools.partial(kernel, ndev, cols),
        out_shape=(jax.ShapeDtypeStruct((3,) + cube, f32), jax.ShapeDtypeStruct((3,) + cube, f32)),
        in_specs=[vmem, vmem, vmem, vmem, vmem, vmem, smem],
        out_specs=(pl.BlockSpec(memory_space=pl.ANY), pl.BlockSpec(memory_space=pl.ANY)),
        scratch_shapes=scratch,
        compiler_params=pltpu.CompilerParams(
            collective_id=0, has_side_effects=True, vmem_limit_bytes=60 * 1024 * 1024
        ),
    )(fields, adjoint, flow, mass, table, numbering, kappa)


def shards(moment_fields, adjoint_fields, velocity, mass_weights, diffusivity, numbering):
    ndev = lax.axis_size("elem")
    cols = ndev // DA
    table = jnp.asarray(shift_tables())
    row_numbers = numbering.reshape(1, -1)
    moments, sensitivities = fused(
        moment_fields, adjoint_fields, velocity, mass_weights, table,
        row_numbers, diffusivity, ndev, cols,
    )
    shape = moment_fields.shape
    return unsort(row_numbers, moments.reshape(shape), sensitivities.reshape(shape))


def solution(mesh):
    in_specs = (
        P(None, None, "elem"),
        P(None, None, "elem"),
        P(None, None, "elem"),
        P(None, "elem"),
        P(),
        P("elem"),
    )
    out_specs = (P(None, None, "elem"), P(None, None, "elem"))
    return jax.shard_map(shards, mesh=mesh, in_specs=in_specs, out_specs=out_specs, check_vma=False)
```
